32 devices in a mesh: groups: 2 (over y), blk: 4 (over z), rep: 4 (over x, core).
Axes of the slice: x: 2, y: 2, z: 4, core: 2. Of those that a mesh axis runs over, the one named last changes fastest.
Arguments:
- orbitals: float32 [8, 262144], P(('groups', 'blk')), parts along dimension 0, may hold values from -6 to 6
- offsets: int32 [8], P('groups'), parts along dimension 0, may hold values from 0 to 3
Outputs:
- exchanged: float32 [8, 262144], P(('groups', 'blk'), 'rep'), parts along dimension 0
- margin: float32 [8, 4], P(('groups', 'blk')), parts along dimension 0
The draws below stay inside these ranges and needn't reach their ends.
There are 2 independent parts, one for each index of `groups`. The reference program is written for one: setup_inputs(seed, part) draws one part's arguments, and reference() takes and returns one part's arrays. A program takes and returns all parts, laid end to end along the dimension named above; each array names one. Nothing has to cross between parts.
All inputs are finite; a program needn't handle non-finite values.
Results may differ from the reference program's by a relative error of at most 0.0001.
Values sent between devices are 32-bit elements; how exact they have to be, the bound alone decides.
A program may use at most 64 MiB of HBM per device.

```python
import jax
import jax.numpy as jnp
from jax import lax

NG = 64
OB = 1
STEPS = 3
NORB = 4
CELLS = 262144
N_BLK = 4
N_REP = 4


def set_ends(drawn, stream_key, smallest, top_value):
    index_at = [jax.random.randint(jax.random.fold_in(stream_key, axis), (), 0, length) for axis, length in enumerate(drawn.shape)]
    widest = drawn.shape.index(max(drawn.shape))
    beside = index_at[:widest] + [(index_at[widest] + 1) % drawn.shape[widest]] + index_at[widest + 1:]
    return drawn.at[tuple(index_at)].set(smallest).at[tuple(beside)].set(top_value)


def level_of(own_key, shape, shards, low, high):
    loudness = 1.0
    for axis_at, parts in shards:
        heights = jax.random.uniform(jax.random.fold_in(jax.random.fold_in(own_key, 6), axis_at), (parts,), jnp.float32, low / len(shards), high / len(shards))
        loudness = loudness * jnp.repeat(jnp.exp(heights), shape[axis_at] // parts).reshape((-1,) + (1,) * (len(shape) - 1 - axis_at))
    return loudness


def centred(stream_key, shape, deviation, reach, split=(), held_as=jnp.bfloat16):
    array = jax.random.normal(stream_key, shape, jnp.float32) * deviation
    if len(split) > 0:
        array = level_of(stream_key, shape, split, -0.22, 0.18) * array
    return jnp.clip(array, min=-reach, max=reach).astype(held_as)


def setup_inputs(seed: int = 0, part: int = 0) -> dict:
    splits = jax.random.split(jax.random.key(seed), 3)
    part_keys = jax.random.split(jax.random.fold_in(splits[2], part), 3)
    orbitals = centred(part_keys[0], (NORB, CELLS), 1.0, 6.0, ((0, 4),), jnp.float32)
    offsets = set_ends(jax.random.randint(part_keys[1], (N_REP,), 0, N_BLK), jax.random.fold_in(part_keys[1], 1), 0, N_BLK - 1).astype(jnp.int32)
    return {"orbitals": orbitals, "offsets": offsets}


precise_mode = lax.Precision.HIGHEST
screen_scale = 0.05


def cas_table(grid_points):
    grid_index = jnp.arange(grid_points, dtype=jnp.int32)
    product = (grid_index[:, None] * grid_index[None, :]) % grid_points
    phase_angle = (2.0 * jnp.pi / grid_points) * product.astype(jnp.float32)
    return jnp.cos(phase_angle) + jnp.sin(phase_angle)


def screened_kernel(grid_points):
    grid_index = jnp.arange(grid_points, dtype=jnp.int32)
    folded = jnp.where(grid_index <= grid_points // 2, grid_index, grid_index - grid_points).astype(jnp.float32)
    squares = folded * folded
    k_squared = squares[:, None, None] + squares[None, :, None] + squares[None, None, :]
    safe_square = jnp.maximum(k_squared, 1.0)
    screened = (4.0 * jnp.pi / (screen_scale * safe_square)) * (1.0 - jnp.exp(-screen_scale * safe_square / (4.0 * jnp.pi)))
    return jnp.where(k_squared > 0.5, screened, jnp.ones_like(screened))


def hartley_cube(values_field, cas_values):
    values_field = jnp.einsum('kx,abxyz->abkyz', cas_values, values_field, precision=precise_mode)
    values_field = jnp.einsum('ky,abxyz->abxkz', cas_values, values_field, precision=precise_mode)
    return jnp.einsum('kz,abxyz->abxyk', cas_values, values_field, precision=precise_mode)


def reference(orbitals, offsets):
    cas_values = cas_table(NG)
    kernel = screened_kernel(NG)
    blocks_all = orbitals.reshape(N_BLK, OB, NG, NG, NG)
    cycle_index = jnp.arange(N_BLK, dtype=jnp.int32)
    accumulator = jnp.zeros_like(blocks_all)

    def one_block(pair_items):
        own_block, vis_block = pair_items
        density = own_block[:, None] * vis_block[None, :]
        potential = hartley_cube(hartley_cube(density, cas_values) * kernel, cas_values) / float(NG ** 3)
        return jnp.sum(potential * vis_block[None, :], axis=1)

    for replica in range(N_REP):
        for step_index in range(STEPS):
            source_block = (cycle_index - offsets[replica] - step_index) % N_BLK
            visiting = jnp.take(blocks_all, source_block.astype(jnp.int32), axis=0)
            accumulator = accumulator + lax.map(one_block, (blocks_all, visiting))
    exchanged = accumulator.reshape(NORB, NG ** 3)
    margin = lax.dot_general(orbitals, exchanged, (((1,), (1,)), ((), ())), precision=precise_mode) / float(NG ** 3)
    return exchanged, margin
```

```python
import functools

import jax
import jax.numpy as jnp
import numpy as np
from jax import lax
from jax.experimental import pallas as pl
from jax.experimental.pallas import tpu as pltpu
from jax.sharding import PartitionSpec as P

NG = 64


precise_mode = lax.Precision.HIGHEST
solve_mode = lax.Precision.HIGH
STEPS = 3
screen_scale = 0.05


def passed_along(block, axis, distance):
    devices = range(lax.axis_size(axis))
    route = [((i - distance) % len(devices), i) for i in devices]
    return lax.ppermute(block, axis, route)


def cas_table(grid_points):
    grid_index = jnp.arange(grid_points, dtype=jnp.int32)
    product = grid_index[:, None] * grid_index[None, :] % grid_points
    phase_angle = 2.0 * jnp.pi / grid_points * product.astype(jnp.float32)
    return jnp.cos(phase_angle) + jnp.sin(phase_angle)


def screened_kernel(grid_points):
    grid_index = jnp.arange(grid_points, dtype=jnp.int32)
    folded = jnp.where(grid_index <= grid_points // 2, grid_index, grid_index - grid_points).astype(
        jnp.float32
    )
    squares = folded * folded
    k_squared = squares[:, None, None] + squares[None, :, None] + squares[None, None, :]
    safe_square = jnp.maximum(k_squared, 1.0)
    screened = (
        4.0
        * jnp.pi
        / (screen_scale * safe_square)
        * (1.0 - jnp.exp(-screen_scale * safe_square / (4.0 * jnp.pi)))
    )
    return jnp.where(k_squared > 0.5, screened, jnp.ones_like(screened))


def transform(values_field, cas_values, cas_paired):
    batch_size = values_field.shape[0]
    grid_points = values_field.shape[1]
    values_field = jnp.einsum(
        "kx,pxq->pkq",
        cas_values,
        values_field.reshape(batch_size, grid_points, grid_points * grid_points),
        precision=solve_mode,
    )
    values_field = jnp.einsum(
        "ky,ayz->akz",
        cas_values,
        values_field.reshape(batch_size * grid_points, grid_points, grid_points),
        precision=solve_mode,
    )
    values_field = jnp.dot(
        values_field.reshape(batch_size * grid_points * grid_points // 2, 2 * grid_points),
        cas_paired,
        precision=solve_mode,
    )
    return values_field.reshape(batch_size, grid_points, grid_points, grid_points)


def cycle_term(own_block, visiting, cas_values, cas_paired, kernel):
    grid_points = kernel.shape[0]
    block_rows = own_block.shape[0]
    density = (own_block[:, None, :] * visiting[None, :, :]).reshape(
        block_rows * block_rows, grid_points, grid_points, grid_points
    )
    spectrum = transform(density, cas_values, cas_paired) * kernel[None]
    potential = transform(spectrum, cas_values, cas_paired).reshape(
        block_rows, block_rows, grid_points**3
    ) / float(grid_points**3)
    return jnp.sum(potential * visiting[None, :, :], axis=1)


def position_block(orbital_block, amount):
    bit_count = (lax.axis_size("blk") - 1).bit_length()
    for bit_level in range(bit_count):
        moved_block = passed_along(orbital_block, "blk", 1 << bit_level)
        orbital_block = jnp.where(amount // (1 << bit_level) % 2 == 1, moved_block, orbital_block)
    return orbital_block


def finish(accumulator, orbitals):
    replica = lax.axis_index("rep")
    exchanged = lax.psum_scatter(accumulator, "rep", scatter_dimension=1, tiled=True)
    quarter_cells = exchanged.shape[1]
    quarter = lax.dynamic_slice_in_dim(orbitals, replica * quarter_cells, quarter_cells, 1)
    slab_orbitals, slab_exchanged = (
        lax.all_to_all(quarter, "blk", split_axis=1, concat_axis=0, tiled=True),
        lax.all_to_all(exchanged, "blk", split_axis=1, concat_axis=0, tiled=True),
    )
    partial_value = lax.dot_general(
        slab_orbitals, slab_exchanged, (((1,), (1,)), ((), ())), precision=precise_mode
    ) / float(NG**3)
    gram_rows = lax.psum_scatter(partial_value, "blk", scatter_dimension=0, tiled=True)
    margin = lax.psum(gram_rows, "rep")
    return (exchanged, margin)


def local_steps(orbitals, offsets):
    cas_values = cas_table(NG)
    cas_paired = jnp.kron(jnp.eye(2, dtype=jnp.float32), cas_values)
    kernel = screened_kernel(NG)
    cycle_size = lax.axis_size("blk")
    replica = lax.axis_index("rep")
    start_block = offsets[replica]
    first_visit = position_block(orbitals, (start_block + 1) % cycle_size)
    behind = passed_along(first_visit, "blk", -1)
    accumulator = cycle_term(orbitals, first_visit, cas_values, cas_paired, kernel)
    ahead_block = passed_along(first_visit, "blk", 1)
    accumulator = accumulator + cycle_term(orbitals, ahead_block, cas_values, cas_paired, kernel)
    accumulator = accumulator + cycle_term(orbitals, behind, cas_values, cas_paired, kernel)
    return finish(accumulator, orbitals)


MESH = pl.DeviceIdType.MESH
LANES = 128


def two_halves(table):
    high = table.astype(jnp.bfloat16)
    low = (table - high.astype(np.float64)).astype(jnp.bfloat16)
    return high, low


def cas_tables(grid_points):
    index = np.arange(grid_points)
    angle = 2.0 * np.pi / grid_points * (np.outer(index, index) % grid_points)
    cas = np.cos(angle) + np.sin(angle)
    high, low = two_halves(np.kron(np.eye(2), cas))
    last_main = np.concatenate([high, high], axis=0)
    blocks = [cas[k::2, y::2] for k in range(2) for y in range(2)]
    y_high, y_low = two_halves(np.concatenate(blocks, axis=0))
    middle = np.concatenate([y_high, y_high, y_low], axis=1)
    x_high, x_low = two_halves(cas)
    first = np.concatenate([x_high, x_high, x_low], axis=1)
    return [jnp.asarray(t) for t in (last_main, low, middle, first)]


def split(values):
    high = values.astype(jnp.bfloat16)
    return high, (values - high.astype(jnp.float32)).astype(jnp.bfloat16)


def dot(a, b):
    return jnp.dot(a, b, preferred_element_type=jnp.float32)


def last_axis(values, main_ref, low_ref):
    high, low = split(values)
    return dot(jnp.concatenate([high, low], axis=1), main_ref[...]) + dot(high, low_ref[...])


def middle_axis(pair, middle_ref):
    half = pair.shape[0]
    high, low = split(pair)
    terms = dot(middle_ref[...], jnp.concatenate([high, low, high], axis=0))
    lane = lax.broadcasted_iota(jnp.int32, (half, pair.shape[1]), 1) % LANES
    first = lane < LANES // 2
    t = [terms[i * half : (i + 1) * half] for i in range(4)]
    straight = jnp.where(first, t[0], t[3])
    crossed = jnp.where(first, t[2], t[1])
    return [
        straight[:, at : at + LANES] + pltpu.roll(crossed[:, at : at + LANES], LANES // 2, 1)
        for at in (0, LANES)
    ]


def first_axis(values, first):
    high, low = split(values)
    return dot(first, jnp.concatenate([high, low, high], axis=0))


def exchange_kernel(
    n,
    pieces,
    offsets_hbm,
    psi_hbm,
    main_hbm,
    low_hbm,
    middle_hbm,
    first_hbm,
    exchanged_ref,
    margin_ref,
    orbs,
    fields,
    given,
    spectra,
    backs,
    back_out,
    table,
    sums,
    gram_out,
    gram_all,
    main_ref,
    low_ref,
    middle_ref,
    first_ref,
    offsets_ref,
    local_sem,
    up_sent,
    down_sent,
    over_sent,
    orb_got,
    swap_sent,
    swap_got,
    back_sent,
    back_got,
    gram_sent,
    gram_got,
):
    b = lax.axis_index("blk")
    r = lax.axis_index("rep")
    slab = orbs.shape[2]
    piece = slab // pieces
    plane = NG * NG // LANES
    slab_planes = slab // plane
    batch = piece // plane
    half = plane // 2
    core = r % 2
    partner = r + 1 - 2 * core
    over = (r + 2) % n
    last = n - 1
    at_edge = (b == 0) | (b == last)
    ticks = (n - 1) * pieces

    barrier = pltpu.get_barrier_semaphore()

    def greet(to):
        pl.semaphore_signal(barrier, inc=1, device_id=to, device_id_type=MESH)

    greet({"rep": partner})
    greet({"rep": over})

    @pl.when(b > 0)
    def _():
        greet({"blk": b - 1})

    @pl.when(b < last)
    def _():
        greet({"blk": b + 1})

    def slab_rows(of):
        return pl.ds(pl.multiple_of(of * slab, slab), slab)

    local = [
        pltpu.make_async_copy(psi_hbm.at[slab_rows(r)], orbs.at[0, b], local_sem.at[0]),
        pltpu.make_async_copy(psi_hbm.at[slab_rows(over)], orbs.at[1, b], local_sem.at[1]),
        pltpu.make_async_copy(main_hbm, main_ref, local_sem.at[2]),
        pltpu.make_async_copy(low_hbm, low_ref, local_sem.at[3]),
        pltpu.make_async_copy(middle_hbm, middle_ref, local_sem.at[4]),
        pltpu.make_async_copy(first_hbm, first_ref, local_sem.at[5]),
        pltpu.make_async_copy(offsets_hbm, offsets_ref, local_sem.at[6]),
    ]
    for copy in local:
        copy.start()

    def folded(index):
        return jnp.where(index <= NG // 2, index, index - NG).astype(jnp.float32)

    lane = lax.broadcasted_iota(jnp.int32, (NG, LANES), 1)
    kx = folded(lax.broadcasted_iota(jnp.int32, (NG, LANES), 0))
    kz = folded(lane % NG)
    base = kx * kx + kz * kz

    def table_rows(k):
        return pl.ds(pl.multiple_of(k * NG, NG), NG)

    def fill(k, _):
        ky = folded(2 * (core * half + k) + lane // NG)
        k_squared = base + ky * ky
        safe = jnp.maximum(k_squared, 1.0)
        scaled = screen_scale * safe / (4.0 * jnp.pi)
        screened = (1.0 - jnp.exp(-scaled)) / scaled
        table[table_rows(k), :] = jnp.where(k_squared > 0.5, screened, 1.0)
        return 0

    lax.fori_loop(0, half, fill, 0)
    exchanged_ref[...] = jnp.zeros_like(exchanged_ref)

    def met(slot):
        s = slot - 1
        edge = s + 1
        inner = jnp.where(s >= 1, s + 1, s)
        low_side = jnp.where(at_edge, edge, inner)
        other = jnp.where(b < n // 2, low_side, last - low_side)
        return jnp.where(slot == 0, b, other)

    def tick_of(t):
        near = 2 * pieces
        slot = jnp.where(at_edge, t // pieces, jnp.where(t < near, t % 2, 2)) + 1
        p = jnp.where(at_edge, t % pieces, jnp.where(t < near, t // 2, t - near))
        return slot, p

    def at_piece(p):
        return pl.ds(pl.multiple_of(p * piece, piece), piece)

    def orb_copy(q_from, q_to, c, p, to, sent):
        return pltpu.make_async_remote_copy(
            src_ref=orbs.at[q_from, c, at_piece(p)],
            dst_ref=orbs.at[q_to, c, at_piece(p)],
            send_sem=sent,
            recv_sem=orb_got.at[q_to, c, p],
            device_id=to,
            device_id_type=MESH,
        )

    def up_copy(q, c, p):
        return orb_copy(q, q, c, p, {"blk": b + 1}, up_sent.at[q, c, p])

    def down_copy(q, c, p):
        return orb_copy(q, q, c, p, {"blk": b - 1}, down_sent.at[q, c, p])

    def over_copy(c, p):
        return orb_copy(0, 1, c, p, {"rep": over}, over_sent.at[c, p])

    def goes_up(q, c):
        wanted = (c <= b) & (b < last)
        return wanted if q == 0 else wanted & (b == 0)

    def goes_down(q, c):
        wanted = (c >= b) & (b > 0)
        return wanted if q == 0 else wanted & (b == last)

    def goes_over(c):
        whole = ((c == 0) & (b == 1)) | ((c == last) & (b == last - 1))
        return (c != b) & jnp.logical_not(whole)

    def forward(q, slot, c, p):
        here = at_piece(p)
        density = orbs[q, b, here, :] * orbs[q, c, here, :]
        turned = last_axis(density, main_ref, low_ref)
        planes = [turned[i * plane : (i + 1) * plane] for i in range(batch)]
        out = []
        for i in range(0, batch, 2):
            pair = jnp.concatenate([planes[i], planes[i + 1]], axis=1)
            out += middle_axis(pair, middle_ref)
        first_half = jnp.concatenate([v[:half] for v in out], axis=0)
        second_half = jnp.concatenate([v[half:] for v in out], axis=0)
        mine = jnp.where(core == 0, first_half, second_half)
        theirs = jnp.where(core == 0, second_half, first_half)
        whose = r if q == 0 else over
        fields[slot, field_rows(whose, p), :] = mine
        given[slot, q, pl.ds(pl.multiple_of(p * batch * half, 8), batch * half), :] = theirs

    def field_rows(of, p):
        start = (of * slab_planes + p * batch) * half
        return pl.ds(pl.multiple_of(start, 8), batch * half)

    def swap_copy(q, slot):
        whose = r if q == 0 else over
        start = pl.multiple_of(whose * slab_planes * half, 8)
        return pltpu.make_async_remote_copy(
            src_ref=given.at[slot, q],
            dst_ref=fields.at[slot, pl.ds(start, slab_planes * half)],
            send_sem=swap_sent.at[slot, q],
            recv_sem=swap_got.at[slot, q],
            device_id={"rep": partner},
            device_id_type=MESH,
        )

    def back_copy(slot):
        return pltpu.make_async_remote_copy(
            src_ref=back_out.at[slot],
            dst_ref=backs.at[slot, core],
            send_sem=back_sent.at[slot],
            recv_sem=back_got.at[slot],
            device_id={"rep": partner},
            device_id_type=MESH,
        )

    wide = 8

    def across(slot):
        for q in range(2):
            swap_copy(q, slot).wait_recv()
        whole = first_ref[...]
        rows = jnp.concatenate(
            [
                first_ref[pl.ds(pl.multiple_of(r * slab_planes, 16), slab_planes), :],
                first_ref[pl.ds(pl.multiple_of(partner * slab_planes, 16), slab_planes), :],
            ],
            axis=0,
        )

        def chunk(i, _):
            k = wide * i
            both = jnp.concatenate(
                [fields[slot, pl.ds(k + w, NG, stride=half), :] for w in range(wide)], axis=1
            )
            factor = jnp.concatenate([table[table_rows(k + w), :] for w in range(wide)], axis=1)
            spectrum = first_axis(both, whole)
            for w in range(wide):
                spectra[slot, table_rows(k + w), :] = spectrum[:, w * LANES : (w + 1) * LANES]
            back = first_axis(spectrum * factor, rows)
            for w in range(wide):
                part = back[:, w * LANES : (w + 1) * LANES]
                places = pl.ds(k + w, slab_planes, stride=half)
                backs[slot, core, places, :] = part[:slab_planes]
                back_out[slot, places, :] = part[slab_planes:]
            return 0

        lax.fori_loop(0, half // wide, chunk, 0)
        back_copy(slot).start()

        def inner(other, _):
            total = jnp.zeros((8, LANES), jnp.float32)
            for k in range(0, half, 4):
                here = pl.ds(k * NG, 4 * NG)
                found = spectra[slot, here, :] * table[here, :] * spectra[other, here, :]
                total = total + jnp.sum(found.reshape(4 * NG // 8, 8, LANES), axis=0)
            sums[slot * n + other] = total
            return 0

        lax.fori_loop(0, slot + 1, inner, 0)

    def weight(distance):
        found = jnp.float32(0.0)
        for replica in range(n):
            for step in range(STEPS):
                found = found + jnp.where((offsets_ref[replica] + step) % n == distance, 1.0, 0.0)
        return found

    def backward(slot):
        c = met(slot)
        scale = weight((b - c + n) % n) / float(NG**3)
        back_copy(slot).wait_recv()

        def one(p, _):
            at = pl.ds(pl.multiple_of(p * batch * half, 8), batch * half)
            first_half = backs[slot, 0, at, :]
            second_half = backs[slot, 1, at, :]
            out = []
            for i in range(0, batch, 2):
                pair = jnp.concatenate(
                    [
                        jnp.concatenate([h[j * half : (j + 1) * half] for h in (first_half, second_half)], axis=0)
                        for j in (i, i + 1)
                    ],
                    axis=1,
                )
                out += middle_axis(pair, middle_ref)
            potential = last_axis(jnp.concatenate(out, axis=0), main_ref, low_ref)
            here = at_piece(p)
            exchanged_ref[here, :] += potential * (orbs[0, c, here, :] * scale)
            return 0

        lax.fori_loop(0, pieces, one, 0)

    for copy in local:
        copy.wait()

    @pl.when(at_edge)
    def _():
        pl.semaphore_wait(barrier, 3)

    @pl.when(jnp.logical_not(at_edge))
    def _():
        pl.semaphore_wait(barrier, 4)

    def send_own(p, _):
        @pl.when(goes_up(0, b))
        def _():
            up_copy(0, b, p).start()

        @pl.when(goes_down(0, b))
        def _():
            down_copy(0, b, p).start()

        return 0

    def send_whole(p, _):
        @pl.when(goes_up(1, b))
        def _():
            up_copy(1, b, p).start()

        @pl.when(goes_down(1, b))
        def _():
            down_copy(1, b, p).start()

        return 0

    lax.fori_loop(0, pieces, send_own, 0)
    lax.fori_loop(0, pieces, send_whole, 0)

    for q in range(2):

        def own_forward(p, _):
            forward(q, 0, b, p)
            return 0

        lax.fori_loop(0, pieces, own_forward, 0)
        swap_copy(q, 0).start()
    across(0)

    lag = jnp.where(at_edge, 2, 2 * pieces)

    def step(t, _):
        @pl.when(t < ticks)
        def _():
            slot, p = tick_of(t)
            c = met(slot)
            orb_copy(0, 0, c, p, {"blk": b}, up_sent.at[0, c, p]).wait_recv()

            @pl.when(goes_up(0, c))
            def _():
                up_copy(0, c, p).start()

            @pl.when(goes_down(0, c))
            def _():
                down_copy(0, c, p).start()

            @pl.when(goes_over(c))
            def _():
                over_copy(c, p).start()

            forward(0, slot, c, p)

            @pl.when(p == pieces - 1)
            def _():
                swap_copy(0, slot).start()

        u = t - lag

        @pl.when(u >= 0)
        def _():
            slot, p = tick_of(u)
            c = met(slot)
            over_copy(c, p).wait_recv()
            forward(1, slot, c, p)

            @pl.when(p == pieces - 1)
            def _():
                swap_copy(1, slot).start()

        @pl.when(t == 1)
        def _():
            backward(0)

        far = u - pieces
        far_slot = jnp.where(at_edge, 1 + far // pieces, far - pieces + 1)
        near_slot = jnp.where(at_edge, 1 + (far - 1) // pieces, far - pieces - 1)

        @pl.when(jnp.where(at_edge, (far >= 0) & (far % pieces == 0), (far == pieces) | (far == pieces + 1)))
        def _():
            across(far_slot)

        @pl.when(jnp.where(at_edge, (far >= 1) & (far % pieces == 1), (far == pieces + 2) | (far == pieces + 3)))
        def _():
            backward(near_slot)

        return 0

    lax.fori_loop(0, ticks + lag, step, 0)
    across(n - 1)

    row = lax.broadcasted_iota(jnp.int32, (n * n, LANES), 0)
    packed = jnp.zeros((n * n, LANES), jnp.float32)
    for slot in range(n):
        for other in range(slot + 1):
            line = jnp.sum(sums[slot * n + other], axis=0, keepdims=True)
            a, c = met(slot), met(other)
            packed = packed + jnp.where((row == a * n + c) | (row == c * n + a), line, 0.0)
    gram_out[...] = packed

    def gram_copy(j, side, source_row, source_core):
        return pltpu.make_async_remote_copy(
            src_ref=gram_out,
            dst_ref=gram_all.at[source_row * 2 + source_core],
            send_sem=gram_sent.at[j * 2 + side],
            recv_sem=gram_got.at[source_row * 2 + source_core],
            device_id={"blk": (b + j) % n, "rep": partner if side else r},
            device_id_type=MESH,
        )

    others = [(j, side) for j in range(n) for side in range(2) if j + side > 0]
    for j, side in others:
        gram_copy(j, side, b, core).start()
    gram_all[b * 2 + core] = packed
    backward(n - 1)

    for j, side in others:
        gram_copy(j, side, (b + j) % n, (core + side) % 2).wait_recv()
    weights = [weight(d) for d in range(n)]
    whole = jnp.zeros((n * n, LANES), jnp.float32)
    for k in range(n):
        distance = (row % n - k + n) % n
        factor = jnp.zeros((n * n, LANES), jnp.float32)
        for d in range(n):
            factor = jnp.where(distance == d, weights[d], factor)
        whole = whole + factor * (gram_all[2 * k] + gram_all[2 * k + 1])
    place = lax.broadcasted_iota(jnp.int32, (1, n), 1)
    answer = jnp.zeros((1, n), jnp.float32)
    for c in range(n):
        value = jnp.sum(jnp.where(row == b * n + c, whole, 0.0)) / float(NG**6)
        answer = jnp.where(place == c, value, answer)
    margin_ref[...] = answer

    for j, side in others:
        gram_copy(j, side, b, core).wait_send()
    for slot in range(n):
        back_copy(slot).wait_send()
        for q in range(2):
            swap_copy(q, slot).wait_send()

    def sent(t, _):
        c = t // pieces
        p = t % pieces
        for q in range(2):

            @pl.when(goes_up(q, c) & ((q == 0) | (c == b)))
            def _():
                up_copy(q, c, p).wait_send()

            @pl.when(goes_down(q, c) & ((q == 0) | (c == b)))
            def _():
                down_copy(q, c, p).wait_send()

        @pl.when(goes_over(c))
        def _():
            over_copy(c, p).wait_send()

        return 0

    lax.fori_loop(0, n * pieces, sent, 0)


def local_distances(orbitals, offsets):
    n = lax.axis_size("blk")
    pieces = 4
    rows = orbitals.shape[1] // LANES
    slab = rows // n
    plane = NG * NG // LANES
    half = plane // 2
    slab_planes = slab // plane
    tables = cas_tables(NG)
    f32 = jnp.float32
    vmem = pl.BlockSpec(memory_space=pltpu.VMEM)
    dma = pltpu.SemaphoreType.DMA
    exchanged, margin = pl.pallas_call(
        functools.partial(exchange_kernel, n, pieces),
        out_shape=(
            jax.ShapeDtypeStruct((slab, LANES), f32),
            jax.ShapeDtypeStruct((1, n), f32),
        ),
        in_specs=[pl.BlockSpec(memory_space=pltpu.HBM)] * 6,
        out_specs=(vmem, vmem),
        scratch_shapes=[
            pltpu.VMEM((2, n, slab, LANES), f32),
            pltpu.VMEM((n, NG * half, LANES), f32),
            pltpu.VMEM((n, 2, slab_planes * half, LANES), f32),
            pltpu.VMEM((n, half * NG, LANES), f32),
            pltpu.VMEM((n, 2, slab_planes * half, LANES), f32),
            pltpu.VMEM((n, slab_planes * half, LANES), f32),
            pltpu.VMEM((half * NG, LANES), f32),
            pltpu.VMEM((n * n, 8, LANES), f32),
            pltpu.VMEM((n * n, LANES), f32),
            pltpu.VMEM((2 * n, n * n, LANES), f32),
            *[pltpu.VMEM(t.shape, t.dtype) for t in tables],
            pltpu.SMEM(offsets.shape, jnp.int32),
            dma((7,)),
            dma((2, n, pieces)),
            dma((2, n, pieces)),
            dma((n, pieces)),
            dma((2, n, pieces)),
            dma((n, 2)),
            dma((n, 2)),
            dma((n,)),
            dma((n,)),
            dma((2 * n,)),
            dma((2 * n,)),
        ],
        compiler_params=pltpu.CompilerParams(
            collective_id=0, has_side_effects=True, vmem_limit_bytes=32 << 20
        ),
    )(offsets, orbitals.reshape(rows, LANES), *tables)
    return exchanged.reshape(1, slab * LANES), margin


def solution(mesh):
    placed = (P(("groups", "blk"), None), P("groups"))
    paired = mesh.shape["blk"] == mesh.shape["rep"] == 4
    local = local_distances if paired else local_steps
    return jax.shard_map(
        local,
        mesh=mesh,
        in_specs=placed,
        out_specs=(P(("groups", "blk"), "rep"), P(("groups", "blk"), None)),
        check_vma=False,
    )
```

```python
import functools

import jax
import jax.numpy as jnp
import numpy as np
from jax import lax
from jax.experimental import pallas as pl
from jax.experimental.pallas import tpu as pltpu
from jax.sharding import PartitionSpec as P

NG = 64


precise_mode = lax.Precision.HIGHEST
solve_mode = lax.Precision.HIGH
STEPS = 3
screen_scale = 0.05


def passed_along(block, axis, distance):
    devices = range(lax.axis_size(axis))
    route = [((i - distance) % len(devices), i) for i in devices]
    return lax.ppermute(block, axis, route)


def cas_table(grid_points):
    grid_index = jnp.arange(grid_points, dtype=jnp.int32)
    product = grid_index[:, None] * grid_index[None, :] % grid_points
    phase_angle = 2.0 * jnp.pi / grid_points * product.astype(jnp.float32)
    return jnp.cos(phase_angle) + jnp.sin(phase_angle)


def screened_kernel(grid_points):
    grid_index = jnp.arange(grid_points, dtype=jnp.int32)
    folded = jnp.where(grid_index <= grid_points // 2, grid_index, grid_index - grid_points).astype(
        jnp.float32
    )
    squares = folded * folded
    k_squared = squares[:, None, None] + squares[None, :, None] + squares[None, None, :]
    safe_square = jnp.maximum(k_squared, 1.0)
    screened = (
        4.0
        * jnp.pi
        / (screen_scale * safe_square)
        * (1.0 - jnp.exp(-screen_scale * safe_square / (4.0 * jnp.pi)))
    )
    return jnp.where(k_squared > 0.5, screened, jnp.ones_like(screened))


def transform(values_field, cas_values, cas_paired):
    batch_size = values_field.shape[0]
    grid_points = values_field.shape[1]
    values_field = jnp.einsum(
        "kx,pxq->pkq",
        cas_values,
        values_field.reshape(batch_size, grid_points, grid_points * grid_points),
        precision=solve_mode,
    )
    values_field = jnp.einsum(
        "ky,ayz->akz",
        cas_values,
        values_field.reshape(batch_size * grid_points, grid_points, grid_points),
        precision=solve_mode,
    )
    values_field = jnp.dot(
        values_field.reshape(batch_size * grid_points * grid_points // 2, 2 * grid_points),
        cas_paired,
        precision=solve_mode,
    )
    return values_field.reshape(batch_size, grid_points, grid_points, grid_points)


def cycle_term(own_block, visiting, cas_values, cas_paired, kernel):
    grid_points = kernel.shape[0]
    block_rows = own_block.shape[0]
    density = (own_block[:, None, :] * visiting[None, :, :]).reshape(
        block_rows * block_rows, grid_points, grid_points, grid_points
    )
    spectrum = transform(density, cas_values, cas_paired) * kernel[None]
    potential = transform(spectrum, cas_values, cas_paired).reshape(
        block_rows, block_rows, grid_points**3
    ) / float(grid_points**3)
    return jnp.sum(potential * visiting[None, :, :], axis=1)


def position_block(orbital_block, amount):
    bit_count = (lax.axis_size("blk") - 1).bit_length()
    for bit_level in range(bit_count):
        moved_block = passed_along(orbital_block, "blk", 1 << bit_level)
        orbital_block = jnp.where(amount // (1 << bit_level) % 2 == 1, moved_block, orbital_block)
    return orbital_block


def finish(accumulator, orbitals):
    replica = lax.axis_index("rep")
    exchanged = lax.psum_scatter(accumulator, "rep", scatter_dimension=1, tiled=True)
    quarter_cells = exchanged.shape[1]
    quarter = lax.dynamic_slice_in_dim(orbitals, replica * quarter_cells, quarter_cells, 1)
    slab_orbitals, slab_exchanged = (
        lax.all_to_all(quarter, "blk", split_axis=1, concat_axis=0, tiled=True),
        lax.all_to_all(exchanged, "blk", split_axis=1, concat_axis=0, tiled=True),
    )
    partial_value = lax.dot_general(
        slab_orbitals, slab_exchanged, (((1,), (1,)), ((), ())), precision=precise_mode
    ) / float(NG**3)
    gram_rows = lax.psum_scatter(partial_value, "blk", scatter_dimension=0, tiled=True)
    margin = lax.psum(gram_rows, "rep")
    return (exchanged, margin)


def local_steps(orbitals, offsets):
    cas_values = cas_table(NG)
    cas_paired = jnp.kron(jnp.eye(2, dtype=jnp.float32), cas_values)
    kernel = screened_kernel(NG)
    cycle_size = lax.axis_size("blk")
    replica = lax.axis_index("rep")
    start_block = offsets[replica]
    first_visit = position_block(orbitals, (start_block + 1) % cycle_size)
    behind = passed_along(first_visit, "blk", -1)
    accumulator = cycle_term(orbitals, first_visit, cas_values, cas_paired, kernel)
    ahead_block = passed_along(first_visit, "blk", 1)
    accumulator = accumulator + cycle_term(orbitals, ahead_block, cas_values, cas_paired, kernel)
    accumulator = accumulator + cycle_term(orbitals, behind, cas_values, cas_paired, kernel)
    return finish(accumulator, orbitals)


MESH = pl.DeviceIdType.MESH
LANES = 128


def two_halves(table):
    high = table.astype(jnp.bfloat16)
    low = (table - high.astype(np.float64)).astype(jnp.bfloat16)
    return high, low


def cas_tables(grid_points):
    index = np.arange(grid_points)
    angle = 2.0 * np.pi / grid_points * (np.outer(index, index) % grid_points)
    cas = np.cos(angle) + np.sin(angle)
    high, low = two_halves(np.kron(np.eye(2), cas))
    last_main = np.concatenate([high, high], axis=0)
    blocks = [cas[k::2, y::2] for k in range(2) for y in range(2)]
    y_high, y_low = two_halves(np.concatenate(blocks, axis=0))
    middle = np.concatenate([y_high, y_high, y_low], axis=1)
    x_high, x_low = two_halves(cas)
    first = np.concatenate([x_high, x_high, x_low], axis=1)
    return [jnp.asarray(t) for t in (last_main, low, middle, first)]


def split(values):
    high = values.astype(jnp.bfloat16)
    return high, (values - high.astype(jnp.float32)).astype(jnp.bfloat16)


def dot(a, b):
    return jnp.dot(a, b, preferred_element_type=jnp.float32)


def last_axis(values, main_ref, low_ref):
    high, low = split(values)
    return dot(jnp.concatenate([high, low], axis=1), main_ref[...]) + dot(high, low_ref[...])


def middle_axis(pair, middle_ref):
    half = pair.shape[0]
    high, low = split(pair)
    terms = dot(middle_ref[...], jnp.concatenate([high, low, high], axis=0))
    lane = lax.broadcasted_iota(jnp.int32, (half, pair.shape[1]), 1) % LANES
    first = lane < LANES // 2
    t = [terms[i * half : (i + 1) * half] for i in range(4)]
    straight = jnp.where(first, t[0], t[3])
    crossed = jnp.where(first, t[2], t[1])
    return [
        straight[:, at : at + LANES] + pltpu.roll(crossed[:, at : at + LANES], LANES // 2, 1)
        for at in (0, LANES)
    ]


def first_axis(values, first):
    high, low = split(values)
    return dot(first, jnp.concatenate([high, low, high], axis=0))


def chosen(index, values):
    found = jnp.int32(values[0])
    for at, value in enumerate(values):
        found = jnp.where(index == at, value, found)
    return found


EDGE_STEPS = (
    (0, (0, 0), None, None),
    (0, (1, 0), 0, None),
    (4, (0, 1), None, 0),
    (6, (1, 1), None, None),
    (7, None, 1, None),
    (8, (0, 2), None, 1),
    (10, (1, 2), None, None),
    (11, None, 2, None),
    (12, (0, 3), None, 2),
    (12, (1, 3), None, None),
    (12, None, 3, 3),
)
INNER_STEPS = (
    (0, (0, 0), None, None),
    (0, (1, 0), 0, None),
    (4, None, None, 0),
    (8, (0, 1), None, None),
    (9, (0, 2), None, None),
    (10, (1, 1), 1, None),
    (11, None, None, 1),
    (12, (0, 3), None, None),
    (12, (1, 2), 2, 2),
    (12, (1, 3), None, None),
    (12, None, 3, 3),
)


def exchange_kernel(
    n,
    pieces,
    offsets_hbm,
    psi_hbm,
    main_hbm,
    low_hbm,
    middle_hbm,
    first_hbm,
    exchanged_ref,
    margin_ref,
    orbs,
    fields,
    spectra,
    backs,
    back_out,
    table,
    gram_out,
    gram_all,
    main_ref,
    low_ref,
    middle_ref,
    first_ref,
    offsets_ref,
    local_sem,
    up_sent,
    down_sent,
    over_sent,
    orb_got,
    rest_got,
    swap_sent,
    swap_got,
    back_sent,
    back_got,
    gram_sent,
    gram_got,
):
    b = lax.axis_index("blk")
    r = lax.axis_index("rep")
    slab = orbs.shape[2]
    piece = slab // pieces
    plane = NG * NG // LANES
    slab_planes = slab // plane
    half = plane // 2
    core = r % 2
    partner = r + 1 - 2 * core
    over = (r + 2) % n
    last = n - 1
    at_edge = (b == 0) | (b == last)

    barrier = pltpu.get_barrier_semaphore()

    def greet(to):
        pl.semaphore_signal(barrier, inc=1, device_id=to, device_id_type=MESH)

    greet({"rep": partner})
    greet({"rep": over})

    @pl.when(b > 0)
    def _():
        greet({"blk": b - 1})

    @pl.when(b < last)
    def _():
        greet({"blk": b + 1})

    def slab_rows(of):
        return pl.ds(pl.multiple_of(of * slab, slab), slab)

    local = [
        pltpu.make_async_copy(psi_hbm.at[slab_rows(r)], orbs.at[0, b], local_sem.at[0]),
        pltpu.make_async_copy(psi_hbm.at[slab_rows(over)], orbs.at[1, b], local_sem.at[1]),
        pltpu.make_async_copy(main_hbm, main_ref, local_sem.at[2]),
        pltpu.make_async_copy(low_hbm, low_ref, local_sem.at[3]),
        pltpu.make_async_copy(middle_hbm, middle_ref, local_sem.at[4]),
        pltpu.make_async_copy(first_hbm, first_ref, local_sem.at[5]),
        pltpu.make_async_copy(offsets_hbm, offsets_ref, local_sem.at[6]),
    ]
    for copy in local:
        copy.start()

    def folded(index):
        return jnp.where(index <= NG // 2, index, index - NG).astype(jnp.float32)

    lane = lax.broadcasted_iota(jnp.int32, (NG, LANES), 1)
    kx = folded(lax.broadcasted_iota(jnp.int32, (NG, LANES), 0))
    kz = folded(lane % NG)
    base = kx * kx + kz * kz

    def table_rows(k):
        return pl.ds(pl.multiple_of(k * NG, NG), NG)

    def fill(k, _):
        ky = folded(2 * (core * half + k) + lane // NG)
        k_squared = base + ky * ky
        safe = jnp.maximum(k_squared, 1.0)
        scaled = screen_scale * safe / (4.0 * jnp.pi)
        screened = (1.0 - jnp.exp(-scaled)) / scaled
        table[table_rows(k), :] = jnp.where(k_squared > 0.5, screened, 1.0)
        return 0

    lax.fori_loop(0, half, fill, 0)
    exchanged_ref[...] = jnp.zeros_like(exchanged_ref)
    gram_out[...] = jnp.zeros_like(gram_out)

    def met(slot):
        edge = slot
        inner = jnp.where(slot == 1, 2, jnp.where(slot == 2, 0, last))
        low_side = jnp.where(at_edge, edge, inner)
        other = jnp.where(b < n // 2, low_side, last - low_side)
        return jnp.where(slot == 0, b, other)

    def tick_of(t):
        near = 2 * pieces
        slot = jnp.where(at_edge, 1 + t // pieces, jnp.where(t < near, 1 + t % 2, 3))
        p = jnp.where(at_edge, t % pieces, jnp.where(t < near, t // 2, t - near))
        return slot, p

    def at_piece(p):
        return pl.ds(pl.multiple_of(p * piece, piece), piece)

    everything = pl.ds(0, slab)

    def orb_copy(q_from, q_to, c, where, got, to, sent):
        return pltpu.make_async_remote_copy(
            src_ref=orbs.at[q_from, c, where],
            dst_ref=orbs.at[q_to, c, where],
            send_sem=sent,
            recv_sem=got,
            device_id=to,
            device_id_type=MESH,
        )

    def got_of(q, c, p):
        return orb_got.at[c, p] if q == 0 else rest_got.at[c]

    def up_copy(q, c, p, where):
        return orb_copy(q, q, c, where, got_of(q, c, p), {"blk": b + 1}, up_sent.at[q, c])

    def down_copy(q, c, p, where):
        return orb_copy(q, q, c, where, got_of(q, c, p), {"blk": b - 1}, down_sent.at[q, c])

    def over_copy(c, where):
        return orb_copy(0, 1, c, where, rest_got.at[c], {"rep": over}, over_sent.at[c])

    def goes_up(q, c):
        wanted = (c <= b) & (b < last)
        return wanted if q == 0 else wanted & (b == 0)

    def goes_down(q, c):
        wanted = (c >= b) & (b > 0)
        return wanted if q == 0 else wanted & (b == last)

    def goes_over(c):
        whole = ((c == 0) & (b == 1)) | ((c == last) & (b == last - 1))
        return (c != b) & jnp.logical_not(whole)

    def middle_all(planes):
        out = []
        for i in range(0, len(planes), 2):
            out += middle_axis(jnp.concatenate(planes[i : i + 2], axis=1), middle_ref)
        return out

    def half_rows(of):
        return pl.ds(pl.multiple_of(of * slab_planes * half, 8), slab_planes * half)

    def forward(q, slot):
        c = met(slot)
        turned = last_axis(orbs[q, b] * orbs[q, c], main_ref, low_ref)
        out = middle_all([turned[i * plane : (i + 1) * plane] for i in range(slab_planes)])
        here = half_rows(jnp.where(q == 0, r, over))
        fields[slot, 0, here, :] = jnp.concatenate([v[:half] for v in out], axis=0)
        fields[slot, 1, here, :] = jnp.concatenate([v[half:] for v in out], axis=0)

    def swap_copy(q, slot):
        here = half_rows(jnp.where(q == 0, r, over))
        return pltpu.make_async_remote_copy(
            src_ref=fields.at[slot, 1 - core, here],
            dst_ref=fields.at[slot, 1 - core, here],
            send_sem=swap_sent.at[slot, q],
            recv_sem=swap_got.at[slot, q],
            device_id={"rep": partner},
            device_id_type=MESH,
        )

    def back_copy(slot):
        return pltpu.make_async_remote_copy(
            src_ref=back_out.at[slot],
            dst_ref=backs.at[slot, core],
            send_sem=back_sent.at[slot],
            recv_sem=back_got.at[slot],
            device_id={"rep": partner},
            device_id_type=MESH,
        )

    def gram_copy(j, side, source_row, source_core):
        return pltpu.make_async_remote_copy(
            src_ref=gram_out,
            dst_ref=gram_all.at[source_row * 2 + source_core],
            send_sem=gram_sent.at[j * 2 + side],
            recv_sem=gram_got.at[source_row * 2 + source_core],
            device_id={"blk": (b + j) % n, "rep": partner if side else r},
            device_id_type=MESH,
        )

    others = [(j, side) for j in range(n) for side in range(2) if j + side > 0]
    row = lax.broadcasted_iota(jnp.int32, (n * n, LANES), 0)

    def across(slot):
        for q in range(2):
            swap_copy(q, slot).wait_recv()
        both = jnp.concatenate(
            [fields[slot, core, pl.ds(k, NG, stride=half), :] for k in range(half)], axis=1
        )
        spectrum = first_axis(both, first_ref[...])
        found = [jnp.zeros((8, LANES), jnp.float32) for _ in range(n)]
        for k in range(half):
            here = slice(k * NG, (k + 1) * NG)
            part = spectrum[:, k * LANES : (k + 1) * LANES]
            spectra[slot, here, :] = part
        for k in range(half):
            here = slice(k * NG, (k + 1) * NG)
            weighted = spectra[slot, here, :] * table[here, :]
            for other in range(n):
                term = weighted * spectra[other, here, :]
                found[other] = found[other] + jnp.sum(term.reshape(NG // 8, 8, LANES), axis=0)
        a = met(slot)
        packed = gram_out[...]
        for other in range(n):
            c = met(other)
            line = jnp.sum(found[other], axis=0, keepdims=True)
            wanted = (other <= slot) & ((row == a * n + c) | (row == c * n + a))
            packed = jnp.where(wanted, line, packed)
        gram_out[...] = packed

        @pl.when(slot == last)
        def _():
            for j, side in others:
                gram_copy(j, side, b, core).start()

        rows = jnp.concatenate(
            [
                first_ref[pl.ds(pl.multiple_of(at * slab_planes, 16), slab_planes), :]
                for at in (r, partner)
            ],
            axis=0,
        )
        weighted = jnp.concatenate(
            [
                spectra[slot, k * NG : (k + 1) * NG, :] * table[k * NG : (k + 1) * NG, :]
                for k in range(half)
            ],
            axis=1,
        )
        back = first_axis(weighted, rows)
        for k in range(half):
            part = back[:, k * LANES : (k + 1) * LANES]
            places = pl.ds(k, slab_planes, stride=half)
            backs[slot, core, places, :] = part[:slab_planes]
            back_out[slot, places, :] = part[slab_planes:]
        back_copy(slot).start()

    def weight(distance):
        found = jnp.float32(0.0)
        for replica in range(n):
            for step in range(STEPS):
                found = found + jnp.where((offsets_ref[replica] + step) % n == distance, 1.0, 0.0)
        return found

    def backward(slot):
        c = met(slot)
        scale = weight((b - c + n) % n) / float(NG**3)
        back_copy(slot).wait_recv()
        sides = [backs[slot, h] for h in range(2)]
        planes = [
            jnp.concatenate([side[i * half : (i + 1) * half] for side in sides], axis=0)
            for i in range(slab_planes)
        ]
        potential = last_axis(jnp.concatenate(middle_all(planes), axis=0), main_ref, low_ref)
        exchanged_ref[...] += potential * (orbs[0, c] * scale)

    for copy in local:
        copy.wait()

    @pl.when(at_edge)
    def _():
        pl.semaphore_wait(barrier, 3)

    @pl.when(jnp.logical_not(at_edge))
    def _():
        pl.semaphore_wait(barrier, 4)

    for q in range(2):

        def send_own(p, _):
            @pl.when(goes_up(q, b))
            def _():
                up_copy(q, b, p, at_piece(p)).start()

            @pl.when(goes_down(q, b))
            def _():
                down_copy(q, b, p, at_piece(p)).start()

            return 0

        lax.fori_loop(0, pieces, send_own, 0)

    def receive(t, _):
        slot, p = tick_of(t)
        c = met(slot)
        up_copy(0, c, p, at_piece(p)).wait_recv()

        @pl.when(goes_up(0, c))
        def _():
            up_copy(0, c, p, at_piece(p)).start()

        @pl.when(goes_down(0, c))
        def _():
            down_copy(0, c, p, at_piece(p)).start()

        @pl.when(goes_over(c))
        def _():
            over_copy(c, at_piece(p)).start()

        return 0

    def planned(i, read):
        return jnp.where(
            at_edge,
            chosen(i, [read(step) for step in EDGE_STEPS]),
            chosen(i, [read(step) for step in INNER_STEPS]),
        )

    def step(i, done):
        upto = planned(i, lambda step: step[0])
        lax.fori_loop(done, upto, receive, 0)
        q = planned(i, lambda step: step[1][0] if step[1] else -1)
        f_slot = planned(i, lambda step: step[1][1] if step[1] else 0)
        a_slot = planned(i, lambda step: -1 if step[2] is None else step[2])
        b_slot = planned(i, lambda step: -1 if step[3] is None else step[3])

        @pl.when((q == 1) & (f_slot > 0))
        def _():
            over_copy(met(f_slot), everything).wait_recv()

        @pl.when(q >= 0)
        def _():
            forward(q, f_slot)
            swap_copy(q, f_slot).start()

        @pl.when(a_slot >= 0)
        def _():
            across(a_slot)

        @pl.when(b_slot >= 0)
        def _():
            backward(b_slot)

        return upto

    lax.fori_loop(0, len(EDGE_STEPS), step, 0)

    for slot in range(n):
        back_copy(slot).wait_send()
        for q in range(2):
            swap_copy(q, slot).wait_send()

    for q in range(2):

        def sent(c, _):
            @pl.when(goes_up(q, c) & ((q == 0) | (c == b)))
            def _():
                up_copy(q, c, 0, everything).wait_send()

            @pl.when(goes_down(q, c) & ((q == 0) | (c == b)))
            def _():
                down_copy(q, c, 0, everything).wait_send()

            if q == 0:

                @pl.when(goes_over(c))
                def _():
                    over_copy(c, everything).wait_send()

            return 0

        lax.fori_loop(0, n, sent, 0)

    gram_all[b * 2 + core] = gram_out[...]
    for j, side in others:
        gram_copy(j, side, (b + j) % n, (core + side) % 2).wait_recv()
    weights = [weight(d) for d in range(n)]
    whole = jnp.zeros((n * n, LANES), jnp.float32)
    for k in range(n):
        distance = (row % n - k + n) % n
        factor = jnp.zeros((n * n, LANES), jnp.float32)
        for d in range(n):
            factor = jnp.where(distance == d, weights[d], factor)
        whole = whole + factor * (gram_all[2 * k] + gram_all[2 * k + 1])
    place = lax.broadcasted_iota(jnp.int32, (1, n), 1)
    answer = jnp.zeros((1, n), jnp.float32)
    for c in range(n):
        value = jnp.sum(jnp.where(row == b * n + c, whole, 0.0)) / float(NG**6)
        answer = jnp.where(place == c, value, answer)
    margin_ref[...] = answer
    for j, side in others:
        gram_copy(j, side, b, core).wait_send()


def local_distances(orbitals, offsets):
    n = lax.axis_size("blk")
    pieces = 4
    rows = orbitals.shape[1] // LANES
    slab = rows // n
    plane = NG * NG // LANES
    half = plane // 2
    slab_planes = slab // plane
    tables = cas_tables(NG)
    f32 = jnp.float32
    vmem = pl.BlockSpec(memory_space=pltpu.VMEM)
    dma = pltpu.SemaphoreType.DMA
    operands = [
        pltpu.with_memory_space_constraint(value, pltpu.HBM)
        for value in (offsets, orbitals.reshape(rows, LANES), *tables)
    ]
    exchanged, margin = pl.pallas_call(
        functools.partial(exchange_kernel, n, pieces),
        out_shape=(
            jax.ShapeDtypeStruct((slab, LANES), f32),
            jax.ShapeDtypeStruct((1, n), f32),
        ),
        in_specs=[pl.BlockSpec(memory_space=pltpu.HBM)] * len(operands),
        out_specs=(vmem, vmem),
        scratch_shapes=[
            pltpu.VMEM((2, n, slab, LANES), f32),
            pltpu.VMEM((n, 2, NG * half, LANES), f32),
            pltpu.VMEM((n, half * NG, LANES), f32),
            pltpu.VMEM((n, 2, slab_planes * half, LANES), f32),
            pltpu.VMEM((n, slab_planes * half, LANES), f32),
            pltpu.VMEM((half * NG, LANES), f32),
            pltpu.VMEM((n * n, LANES), f32),
            pltpu.VMEM((2 * n, n * n, LANES), f32),
            *[pltpu.VMEM(t.shape, t.dtype) for t in tables],
            pltpu.SMEM(offsets.shape, jnp.int32),
            dma((7,)),
            dma((2, n)),
            dma((2, n)),
            dma((n,)),
            dma((n, pieces)),
            dma((n,)),
            dma((n, 2)),
            dma((n, 2)),
            dma((n,)),
            dma((n,)),
            dma((2 * n,)),
            dma((2 * n,)),
        ],
        compiler_params=pltpu.CompilerParams(
            collective_id=0, has_side_effects=True, vmem_limit_bytes=32 << 20
        ),
    )(*operands)
    return exchanged.reshape(1, slab * LANES), margin


def solution(mesh):
    placed = (P(("groups", "blk"), None), P("groups"))
    paired = mesh.shape["blk"] == mesh.shape["rep"] == 4
    local = local_distances if paired else local_steps
    return jax.shard_map(
        local,
        mesh=mesh,
        in_specs=placed,
        out_specs=(P(("groups", "blk"), "rep"), P(("groups", "blk"), None)),
        check_vma=False,
    )
```

```python
import functools

import jax
import jax.numpy as jnp
import numpy as np
from jax import lax
from jax.experimental import pallas as pl
from jax.experimental.pallas import tpu as pltpu
from jax.sharding import PartitionSpec as P

NG = 64


precise_mode = lax.Precision.HIGHEST
solve_mode = lax.Precision.HIGH
STEPS = 3
screen_scale = 0.05


def passed_along(block, axis, distance):
    devices = range(lax.axis_size(axis))
    route = [((i - distance) % len(devices), i) for i in devices]
    return lax.ppermute(block, axis, route)


def cas_table(grid_points):
    grid_index = jnp.arange(grid_points, dtype=jnp.int32)
    product = grid_index[:, None] * grid_index[None, :] % grid_points
    phase_angle = 2.0 * jnp.pi / grid_points * product.astype(jnp.float32)
    return jnp.cos(phase_angle) + jnp.sin(phase_angle)


def screened_kernel(grid_points):
    grid_index = jnp.arange(grid_points, dtype=jnp.int32)
    folded = jnp.where(grid_index <= grid_points // 2, grid_index, grid_index - grid_points).astype(
        jnp.float32
    )
    squares = folded * folded
    k_squared = squares[:, None, None] + squares[None, :, None] + squares[None, None, :]
    safe_square = jnp.maximum(k_squared, 1.0)
    screened = (
        4.0
        * jnp.pi
        / (screen_scale * safe_square)
        * (1.0 - jnp.exp(-screen_scale * safe_square / (4.0 * jnp.pi)))
    )
    return jnp.where(k_squared > 0.5, screened, jnp.ones_like(screened))


def transform(values_field, cas_values, cas_paired):
    batch_size = values_field.shape[0]
    grid_points = values_field.shape[1]
    values_field = jnp.einsum(
        "kx,pxq->pkq",
        cas_values,
        values_field.reshape(batch_size, grid_points, grid_points * grid_points),
        precision=solve_mode,
    )
    values_field = jnp.einsum(
        "ky,ayz->akz",
        cas_values,
        values_field.reshape(batch_size * grid_points, grid_points, grid_points),
        precision=solve_mode,
    )
    values_field = jnp.dot(
        values_field.reshape(batch_size * grid_points * grid_points // 2, 2 * grid_points),
        cas_paired,
        precision=solve_mode,
    )
    return values_field.reshape(batch_size, grid_points, grid_points, grid_points)


def cycle_term(own_block, visiting, cas_values, cas_paired, kernel):
    grid_points = kernel.shape[0]
    block_rows = own_block.shape[0]
    density = (own_block[:, None, :] * visiting[None, :, :]).reshape(
        block_rows * block_rows, grid_points, grid_points, grid_points
    )
    spectrum = transform(density, cas_values, cas_paired) * kernel[None]
    potential = transform(spectrum, cas_values, cas_paired).reshape(
        block_rows, block_rows, grid_points**3
    ) / float(grid_points**3)
    return jnp.sum(potential * visiting[None, :, :], axis=1)


def position_block(orbital_block, amount):
    bit_count = (lax.axis_size("blk") - 1).bit_length()
    for bit_level in range(bit_count):
        moved_block = passed_along(orbital_block, "blk", 1 << bit_level)
        orbital_block = jnp.where(amount // (1 << bit_level) % 2 == 1, moved_block, orbital_block)
    return orbital_block


def finish(accumulator, orbitals):
    replica = lax.axis_index("rep")
    exchanged = lax.psum_scatter(accumulator, "rep", scatter_dimension=1, tiled=True)
    quarter_cells = exchanged.shape[1]
    quarter = lax.dynamic_slice_in_dim(orbitals, replica * quarter_cells, quarter_cells, 1)
    slab_orbitals, slab_exchanged = (
        lax.all_to_all(quarter, "blk", split_axis=1, concat_axis=0, tiled=True),
        lax.all_to_all(exchanged, "blk", split_axis=1, concat_axis=0, tiled=True),
    )
    partial_value = lax.dot_general(
        slab_orbitals, slab_exchanged, (((1,), (1,)), ((), ())), precision=precise_mode
    ) / float(NG**3)
    gram_rows = lax.psum_scatter(partial_value, "blk", scatter_dimension=0, tiled=True)
    margin = lax.psum(gram_rows, "rep")
    return (exchanged, margin)


def local_steps(orbitals, offsets):
    cas_values = cas_table(NG)
    cas_paired = jnp.kron(jnp.eye(2, dtype=jnp.float32), cas_values)
    kernel = screened_kernel(NG)
    cycle_size = lax.axis_size("blk")
    replica = lax.axis_index("rep")
    start_block = offsets[replica]
    first_visit = position_block(orbitals, (start_block + 1) % cycle_size)
    behind = passed_along(first_visit, "blk", -1)
    accumulator = cycle_term(orbitals, first_visit, cas_values, cas_paired, kernel)
    ahead_block = passed_along(first_visit, "blk", 1)
    accumulator = accumulator + cycle_term(orbitals, ahead_block, cas_values, cas_paired, kernel)
    accumulator = accumulator + cycle_term(orbitals, behind, cas_values, cas_paired, kernel)
    return finish(accumulator, orbitals)


MESH = pl.DeviceIdType.MESH
LANES = 128


def two_halves(table):
    high = table.astype(jnp.bfloat16)
    low = (table - high.astype(np.float64)).astype(jnp.bfloat16)
    return high, low


def cas_tables(grid_points):
    index = np.arange(grid_points)
    angle = 2.0 * np.pi / grid_points * (np.outer(index, index) % grid_points)
    cas = np.cos(angle) + np.sin(angle)
    high, low = two_halves(np.kron(np.eye(2), cas))
    last_main = np.concatenate([high, high], axis=0)
    blocks = [cas[k::2, y::2] for k in range(2) for y in range(2)]
    y_high, y_low = two_halves(np.concatenate(blocks, axis=0))
    middle = np.concatenate([y_high, y_high, y_low], axis=1)
    x_high, x_low = two_halves(cas)
    first = np.concatenate([x_high, x_high, x_low], axis=1)
    return [jnp.asarray(t) for t in (last_main, low, middle, first)]


def split(values):
    high = values.astype(jnp.bfloat16)
    return high, (values - high.astype(jnp.float32)).astype(jnp.bfloat16)


def dot(a, b):
    return jnp.dot(a, b, preferred_element_type=jnp.float32)


def last_axis(values, main_ref, low_ref):
    high, low = split(values)
    return dot(jnp.concatenate([high, low], axis=1), main_ref[...]) + dot(high, low_ref[...])


def middle_axis(pair, middle_ref):
    half = pair.shape[0]
    high, low = split(pair)
    terms = dot(middle_ref[...], jnp.concatenate([high, low, high], axis=0))
    lane = lax.broadcasted_iota(jnp.int32, (half, pair.shape[1]), 1) % LANES
    first = lane < LANES // 2
    t = [terms[i * half : (i + 1) * half] for i in range(4)]
    straight = jnp.where(first, t[0], t[3])
    crossed = jnp.where(first, t[2], t[1])
    return [
        straight[:, at : at + LANES] + pltpu.roll(crossed[:, at : at + LANES], LANES // 2, 1)
        for at in (0, LANES)
    ]


def first_axis(values, first):
    high, low = split(values)
    return dot(first, jnp.concatenate([high, low, high], axis=0))


def chosen(index, values):
    found = jnp.int32(values[0])
    for at, value in enumerate(values):
        found = jnp.where(index == at, value, found)
    return found


EDGE_STEPS = (
    (0, (0, 0), None, None, 0),
    (0, (1, 0), (0, 0, 2), 0, 0),
    (8, (0, 1), None, None, 0),
    (12, (1, 1), None, None, 0),
    (15, None, (1, 0, 1), None, 0),
    (16, (0, 2), (1, 1, 2), 1, 1),
    (16, (1, 2), (2, 0, 2), 2, 0),
)
INNER_STEPS = (
    (0, (0, 0), None, None, 0),
    (0, (1, 0), None, None, 0),
    (2, None, (0, 0, 1), None, 0),
    (4, None, (0, 1, 2), None, 0),
    (6, None, None, 0, 0),
    (16, (0, 1), None, None, 0),
    (17, (0, 2), None, None, 0),
    (22, (1, 1), None, None, 0),
    (23, (1, 2), None, None, 0),
    (24, None, (1, 0, 2), 1, 0),
    (24, (0, 3), (2, 0, 2), 2, 1),
    (24, (1, 3), (3, 0, 2), 3, 0),
)
EDGE_ORDER = (0, 2, 3, 1)
INNER_ORDER = (1, 0, 2, 3)


def exchange_kernel(
    n,
    pieces,
    shared,
    offsets_hbm,
    psi_hbm,
    main_hbm,
    low_hbm,
    middle_hbm,
    first_hbm,
    exchanged_ref,
    margin_ref,
    orbs,
    fields,
    back_ref,
    pots,
    table,
    square,
    term_out,
    term_in,
    gram_out,
    gram_all,
    main_ref,
    low_ref,
    middle_ref,
    first_ref,
    offsets_ref,
    local_sem,
    up_sent,
    down_sent,
    over_sent,
    orb_got,
    rest_got,
    swap_sent,
    swap_got,
    term_sem,
    gram_sem,
):
    b = lax.axis_index("blk")
    r = lax.axis_index("rep")
    slab = orbs.shape[2]
    piece = slab // pieces
    plane = NG * NG // LANES
    slab_planes = slab // plane
    core = r % 2
    partner = r + 1 - 2 * core
    over = (r + 2) % n
    last = n - 1
    at_edge = (b == 0) | (b == last)
    edge = jnp.where(b < n // 2, 0, last)

    barrier = pltpu.get_barrier_semaphore()

    def greet(to):
        pl.semaphore_signal(barrier, inc=1, device_id=to, device_id_type=MESH)

    for j in range(1, n):
        greet({"rep": (r + j) % n})

    @pl.when(b > 0)
    def _():
        greet({"blk": b - 1})

    @pl.when(b < last)
    def _():
        greet({"blk": b + 1})

    def slab_rows(of):
        return pl.ds(pl.multiple_of(of * slab, slab), slab)

    local = [
        pltpu.make_async_copy(psi_hbm.at[slab_rows(r)], orbs.at[0, b], local_sem.at[0]),
        pltpu.make_async_copy(psi_hbm.at[slab_rows(over)], orbs.at[1, b], local_sem.at[1]),
        pltpu.make_async_copy(main_hbm, main_ref, local_sem.at[2]),
        pltpu.make_async_copy(low_hbm, low_ref, local_sem.at[3]),
        pltpu.make_async_copy(middle_hbm, middle_ref, local_sem.at[4]),
        pltpu.make_async_copy(first_hbm, first_ref, local_sem.at[5]),
        pltpu.make_async_copy(offsets_hbm, offsets_ref, local_sem.at[6]),
    ]
    for copy in local:
        copy.start()

    def folded(index):
        return jnp.where(index <= NG // 2, index, index - NG).astype(jnp.float32)

    lane = lax.broadcasted_iota(jnp.int32, (NG, LANES), 1)
    kx = folded(lax.broadcasted_iota(jnp.int32, (NG, LANES), 0))
    kz = folded(lane % NG)
    base = kx * kx + kz * kz

    def fill(k, _):
        ky = folded(2 * k + lane // NG)
        k_squared = base + ky * ky
        safe = jnp.maximum(k_squared, 1.0)
        scaled = screen_scale * safe / (4.0 * jnp.pi)
        screened = (1.0 - jnp.exp(-scaled)) / scaled
        here = pl.ds(pl.multiple_of(k * NG, NG), NG)
        table[here, :] = jnp.where(k_squared > 0.5, screened, 1.0)
        return 0


    def met(slot):
        low_side = jnp.where(at_edge, chosen(slot, EDGE_ORDER), chosen(slot, INNER_ORDER))
        return jnp.where(b < n // 2, low_side, last - low_side)

    def tick_of(t):
        near = 2 * pieces
        slot = jnp.where(at_edge, 1 + t // pieces, jnp.where(t < near, 1 + t % 2, 3))
        p = jnp.where(at_edge, t % pieces, jnp.where(t < near, t // 2, t - near))
        return slot, p

    def at_piece(p):
        return pl.ds(pl.multiple_of(p * piece, piece), piece)

    everything = pl.ds(0, slab)
    by_x = pl.ds(0, shared * piece)
    by_z = pl.ds(shared * piece, slab - shared * piece)

    def orb_copy(q_from, q_to, c, where, got, to, sent):
        return pltpu.make_async_remote_copy(
            src_ref=orbs.at[q_from, c, where],
            dst_ref=orbs.at[q_to, c, where],
            send_sem=sent,
            recv_sem=got,
            device_id=to,
            device_id_type=MESH,
        )

    def got_of(q, c, p):
        return orb_got.at[c, p] if q == 0 else rest_got.at[c]

    def up_copy(q, c, p, where):
        return orb_copy(q, q, c, where, got_of(q, c, p), {"blk": b + 1}, up_sent.at[q, c])

    def down_copy(q, c, p, where):
        return orb_copy(q, q, c, where, got_of(q, c, p), {"blk": b - 1}, down_sent.at[q, c])

    def over_copy(c, where):
        return orb_copy(0, 1, c, where, rest_got.at[c], {"rep": over}, over_sent.at[c])

    def goes_up(c):
        return (c <= b) & (b < last) & jnp.logical_not((c == b) & (b + 1 == last))

    def goes_down(c):
        return (c >= b) & (b > 0) & jnp.logical_not((c == b) & (b == 1))

    def halved(c):
        return ((c == 0) & (b == 1)) | ((c == last) & (b == last - 1))

    def comes(c):
        return (c != b) & jnp.logical_not(at_edge & (c == met(last)))

    def middle_all(planes):
        out = []
        for i in range(0, len(planes), 2):
            out += middle_axis(jnp.concatenate(planes[i : i + 2], axis=1), middle_ref)
        return jnp.concatenate(out, axis=0)

    def planes_of(values):
        return [values[i * plane : (i + 1) * plane] for i in range(slab_planes)]

    def forward(q, slot):
        c = met(slot)
        turned = last_axis(orbs[q, b] * orbs[q, c], main_ref, low_ref)
        fields[slot, slab_rows(jnp.where(q == 0, r, over)), :] = middle_all(planes_of(turned))

    def swap_copy(q, slot):
        here = slab_rows(jnp.where(q == 0, r, over))
        return pltpu.make_async_remote_copy(
            src_ref=fields.at[slot, here],
            dst_ref=fields.at[slot, here],
            send_sem=swap_sent.at[slot, q],
            recv_sem=swap_got.at[slot, q],
            device_id={"rep": partner},
            device_id_type=MESH,
        )

    def across(slot, part):
        wide = plane // 2
        start = part * wide

        @pl.when(part == 0)
        def _():
            for q in range(2):
                swap_copy(q, slot).wait_recv()
            square[...] = jnp.zeros_like(square)

        rows = first_ref[pl.ds(pl.multiple_of(r * slab_planes, 16), slab_planes), :]
        both = jnp.concatenate(
            [fields[slot, pl.ds(start + k, NG, stride=plane), :] for k in range(wide)], axis=1
        )
        factor = jnp.concatenate(
            [table[pl.ds(pl.multiple_of((start + k) * NG, NG), NG), :] for k in range(wide)], axis=1
        )
        spectrum = first_axis(both, first_ref[...])
        weighted = spectrum * factor
        folds = jnp.sum((spectrum * weighted).reshape(NG // 8, 8, wide * LANES), axis=0)
        total = square[...]
        for k in range(wide):
            total = total + folds[:, k * LANES : (k + 1) * LANES]
        square[...] = total
        back = first_axis(weighted, rows)
        for k in range(wide):
            places = pl.ds(start + k, slab_planes, stride=plane)
            back_ref[places, :] = back[:, k * LANES : (k + 1) * LANES]

    def weight(distance):
        found = jnp.float32(0.0)
        for replica in range(n):
            for step in range(STEPS):
                found = found + jnp.where((offsets_ref[replica] + step) % n == distance, 1.0, 0.0)
        return found

    def weight_of(c, k):
        return weight((c - k + n) % n)

    def term_copy():
        return pltpu.make_async_remote_copy(
            src_ref=term_out,
            dst_ref=term_in,
            send_sem=term_sem.at[0],
            recv_sem=term_sem.at[1],
            device_id={"blk": edge},
            device_id_type=MESH,
        )

    def backward(slot):
        c = met(slot)
        scale = weight_of(b, c) / float(NG**3)
        potential = last_axis(middle_all(planes_of(back_ref[...])), main_ref, low_ref)
        pots[slot] = potential
        exchanged_ref[...] += potential * (orbs[0, c] * scale)

        @pl.when((slot == 1) & jnp.logical_not(at_edge))
        def _():
            there = weight_of(edge, b) / float(NG**3)
            term_out[...] = pots[1] * (orbs[0, b] * there)
            term_copy().start()

    row = lax.broadcasted_iota(jnp.int32, (n * n, LANES), 0)
    me = b * n + r

    def gram_copy(j, source):
        to = (me + j) % (n * n)
        return pltpu.make_async_remote_copy(
            src_ref=gram_out,
            dst_ref=gram_all.at[source],
            send_sem=gram_sem.at[0],
            recv_sem=gram_sem.at[1],
            device_id={"blk": to // n, "rep": to % n},
            device_id_type=MESH,
        )

    def every_gram():
        return pltpu.make_async_remote_copy(
            src_ref=gram_all.at[pl.ds(1, n * n - 1)],
            dst_ref=gram_all.at[pl.ds(1, n * n - 1)],
            send_sem=gram_sem.at[0],
            recv_sem=gram_sem.at[1],
            device_id={"rep": partner},
            device_id_type=MESH,
        )

    combos = [(i, j) for i in range(n - 1) for j in range(i, n)]

    def margin_terms():
        block = 32

        def one(t, sums):
            here = pl.ds(pl.multiple_of(t * block, block), block)
            met_orbs = [orbs[0, met(slot), here, :] for slot in range(n)]
            found = [pots[slot, here, :] for slot in range(n - 1)]
            own = [met_orbs[0] * v for v in met_orbs]
            theirs = [met_orbs[1] * v for v in met_orbs]
            terms = [found[i] * own[j] for i, j in combos] + [found[1] * v for v in theirs]
            return tuple(
                total + jnp.sum(term.reshape(block // 8, 8, LANES), axis=0)
                for total, term in zip(sums, terms)
            )

        zero = jnp.zeros((8, LANES), jnp.float32)
        sums = lax.fori_loop(0, slab // block, one, (zero,) * (len(combos) + n))
        packed = jnp.zeros((n * n, LANES), jnp.float32)

        def added(packed, line, wanted, a, c, k):
            spot = (row == a * n + c) & wanted
            return packed + jnp.where(spot, line * weight_of(c, k), 0.0)

        always = jnp.logical_not(at_edge)
        for at, (i, j) in enumerate(combos):
            wanted = always if i > 1 or j > 2 else jnp.bool_(True)
            line = jnp.sum(sums[at], axis=0, keepdims=True)
            a, c = met(i), met(j)
            packed = added(packed, line, wanted, a, c, b)
            if i != j:
                packed = added(packed, line, wanted, c, a, b)
            elif i == 1:
                packed = added(packed, line, at_edge, b, b, a)
        for j in range(n):
            line = jnp.sum(sums[len(combos) + j], axis=0, keepdims=True)
            a, k = met(j), met(1)
            packed = added(packed, line, always, a, b, k)
            if j != 0:
                packed = added(packed, line, always, b, a, k)
        gram_out[...] = packed
        for j in range(1, n * n):
            gram_copy(j, me).start()

    exchanged_ref[...] = jnp.zeros_like(exchanged_ref)
    for copy in local:
        copy.wait()

    @pl.when(at_edge)
    def _():
        pl.semaphore_wait(barrier, n)

    @pl.when(jnp.logical_not(at_edge))
    def _():
        pl.semaphore_wait(barrier, n + 1)

    def send_own(p, _):
        @pl.when(goes_up(b))
        def _():
            up_copy(0, b, p, at_piece(p)).start()

        @pl.when(goes_down(b))
        def _():
            down_copy(0, b, p, at_piece(p)).start()

        return 0

    lax.fori_loop(0, pieces, send_own, 0)

    @pl.when(b == 0)
    def _():
        up_copy(1, b, 0, by_z).start()

    @pl.when(b == last)
    def _():
        down_copy(1, b, 0, by_z).start()


    def receive(t, _):
        slot, p = tick_of(t)
        c = met(slot)
        up_copy(0, c, p, at_piece(p)).wait_recv()

        @pl.when(goes_up(c))
        def _():
            up_copy(0, c, p, at_piece(p)).start()

        @pl.when(goes_down(c))
        def _():
            down_copy(0, c, p, at_piece(p)).start()

        @pl.when(jnp.logical_not(halved(c)) | (p < shared))
        def _():
            over_copy(c, at_piece(p)).start()

        return 0

    def swapped(slot, _):
        for q in range(2):
            swap_copy(q, slot).wait_send()
        return 0

    def sent(c, _):
        @pl.when(goes_up(c))
        def _():
            up_copy(0, c, 0, everything).wait_send()

        @pl.when(goes_down(c))
        def _():
            down_copy(0, c, 0, everything).wait_send()

        @pl.when(comes(c) & halved(c))
        def _():
            over_copy(c, by_x).wait_send()

        @pl.when(comes(c) & jnp.logical_not(halved(c)))
        def _():
            over_copy(c, everything).wait_send()

        return 0

    def orbitals_sent():
        lax.fori_loop(0, jnp.where(at_edge, n - 2, last), swapped, 0)
        lax.fori_loop(0, n, sent, 0)

        @pl.when(b == 0)
        def _():
            up_copy(1, b, 0, by_z).wait_send()

        @pl.when(b == last)
        def _():
            down_copy(1, b, 0, by_z).wait_send()

    def planned(i, read):
        return jnp.where(
            at_edge,
            chosen(i, [read(step) for step in EDGE_STEPS]),
            chosen(i, [read(step) for step in INNER_STEPS]),
        )

    steps = jnp.where(at_edge, len(EDGE_STEPS), len(INNER_STEPS))

    def step(i, done):
        upto = planned(i, lambda step: step[0] * pieces // 8)
        lax.fori_loop(done, upto, receive, 0)
        q = planned(i, lambda step: step[1][0] if step[1] else -1)
        f_slot = planned(i, lambda step: step[1][1] if step[1] else 0)
        a_slot = planned(i, lambda step: step[2][0] if step[2] else 0)
        a_from = planned(i, lambda step: step[2][1] if step[2] else 0)
        a_to = planned(i, lambda step: step[2][2] if step[2] else 0)
        b_slot = planned(i, lambda step: -1 if step[3] is None else step[3])
        adds = planned(i, lambda step: step[4])

        @pl.when(i == steps - 1)
        def _():
            orbitals_sent()

        @pl.when((q == 1) & (f_slot > 0))
        def _():
            over_copy(met(f_slot), everything).wait_recv()

        @pl.when(q >= 0)
        def _():
            forward(q, f_slot)
            swap_copy(q, f_slot).start()

        @pl.when(i == 1)
        def _():
            lax.fori_loop(0, plane, fill, 0)

        def one_across(part, _):
            across(a_slot, part)
            return 0

        lax.fori_loop(a_from, a_to, one_across, 0)

        @pl.when(b_slot >= 0)
        def _():
            backward(b_slot)

        @pl.when(adds == 1)
        def _():
            margin_terms()

        return upto

    lax.fori_loop(0, steps, step, jnp.int32(0))

    for q in range(2):
        swap_copy(q, jnp.where(at_edge, n - 2, last)).wait_send()

    gram_all[me] = gram_out[...]
    every_gram().wait_recv()
    whole = gram_all[0]
    for k in range(1, n * n):
        whole = whole + gram_all[k]
    line = jnp.sum(square[...], axis=0, keepdims=True) * weight_of(b, met(2))
    whole = whole + jnp.where((row == b * n + b) & at_edge, line, 0.0)
    sums = jnp.sum(whole, axis=1, keepdims=True) / float(NG**6)
    at_row = lax.broadcasted_iota(jnp.int32, (n * n, n), 0)
    at_lane = lax.broadcasted_iota(jnp.int32, (n * n, n), 1)
    kept = jnp.where(at_row == b * n + at_lane, sums, 0.0)
    margin_ref[...] = jnp.sum(kept, axis=0, keepdims=True)

    @pl.when(at_edge)
    def _():
        term_copy().wait_recv()
        exchanged_ref[...] += term_in[...]

    @pl.when(jnp.logical_not(at_edge))
    def _():
        term_copy().wait_send()

    every_gram().wait_send()


def local_distances(orbitals, offsets):
    n = lax.axis_size("blk")
    pieces = 4
    shared = 1
    rows = orbitals.shape[1] // LANES
    slab = rows // n
    plane = NG * NG // LANES
    tables = cas_tables(NG)
    f32 = jnp.float32
    vmem = pl.BlockSpec(memory_space=pltpu.VMEM)
    dma = pltpu.SemaphoreType.DMA
    operands = [
        pltpu.with_memory_space_constraint(value, pltpu.HBM)
        for value in (offsets, orbitals.reshape(rows, LANES), *tables)
    ]
    exchanged, margin = pl.pallas_call(
        functools.partial(exchange_kernel, n, pieces, shared),
        out_shape=(
            jax.ShapeDtypeStruct((slab, LANES), f32),
            jax.ShapeDtypeStruct((1, n), f32),
        ),
        in_specs=[pl.BlockSpec(memory_space=pltpu.HBM)] * len(operands),
        out_specs=(vmem, vmem),
        scratch_shapes=[
            pltpu.VMEM((2, n, slab, LANES), f32),
            pltpu.VMEM((n, rows, LANES), f32),
            pltpu.VMEM((slab, LANES), f32),
            pltpu.VMEM((n, slab, LANES), f32),
            pltpu.VMEM((plane * NG, LANES), f32),
            pltpu.VMEM((8, LANES), f32),
            pltpu.VMEM((slab, LANES), f32),
            pltpu.VMEM((slab, LANES), f32),
            pltpu.VMEM((n * n, LANES), f32),
            pltpu.VMEM((n * n, n * n, LANES), f32),
            *[pltpu.VMEM(t.shape, t.dtype) for t in tables],
            pltpu.SMEM(offsets.shape, jnp.int32),
            dma((7,)),
            dma((2, n)),
            dma((2, n)),
            dma((n,)),
            dma((n, pieces)),
            dma((n,)),
            dma((n, 2)),
            dma((n, 2)),
            dma((2,)),
            dma((2,)),
        ],
        compiler_params=pltpu.CompilerParams(
            collective_id=0, has_side_effects=True, vmem_limit_bytes=32 << 20
        ),
    )(*operands)
    return exchanged.reshape(1, slab * LANES), margin


def solution(mesh):
    placed = (P(("groups", "blk"), None), P("groups"))
    paired = mesh.shape["blk"] == mesh.shape["rep"] == 4
    local = local_distances if paired else local_steps
    return jax.shard_map(
        local,
        mesh=mesh,
        in_specs=placed,
        out_specs=(P(("groups", "blk"), "rep"), P(("groups", "blk"), None)),
        check_vma=False,
    )
```

```python
import functools

import jax
import jax.numpy as jnp
import numpy as np
from jax import lax
from jax.experimental import pallas as pl
from jax.experimental.pallas import tpu as pltpu
from jax.sharding import PartitionSpec as P

NG = 64


precise_mode = lax.Precision.HIGHEST
solve_mode = lax.Precision.HIGH
STEPS = 3
screen_scale = 0.05


def passed_along(block, axis, distance):
    devices = range(lax.axis_size(axis))
    route = [((i - distance) % len(devices), i) for i in devices]
    return lax.ppermute(block, axis, route)


def cas_table(grid_points):
    grid_index = jnp.arange(grid_points, dtype=jnp.int32)
    product = grid_index[:, None] * grid_index[None, :] % grid_points
    phase_angle = 2.0 * jnp.pi / grid_points * product.astype(jnp.float32)
    return jnp.cos(phase_angle) + jnp.sin(phase_angle)


def screened_kernel(grid_points):
    grid_index = jnp.arange(grid_points, dtype=jnp.int32)
    folded = jnp.where(grid_index <= grid_points // 2, grid_index, grid_index - grid_points).astype(
        jnp.float32
    )
    squares = folded * folded
    k_squared = squares[:, None, None] + squares[None, :, None] + squares[None, None, :]
    safe_square = jnp.maximum(k_squared, 1.0)
    screened = (
        4.0
        * jnp.pi
        / (screen_scale * safe_square)
        * (1.0 - jnp.exp(-screen_scale * safe_square / (4.0 * jnp.pi)))
    )
    return jnp.where(k_squared > 0.5, screened, jnp.ones_like(screened))


def transform(values_field, cas_values, cas_paired):
    batch_size = values_field.shape[0]
    grid_points = values_field.shape[1]
    values_field = jnp.einsum(
        "kx,pxq->pkq",
        cas_values,
        values_field.reshape(batch_size, grid_points, grid_points * grid_points),
        precision=solve_mode,
    )
    values_field = jnp.einsum(
        "ky,ayz->akz",
        cas_values,
        values_field.reshape(batch_size * grid_points, grid_points, grid_points),
        precision=solve_mode,
    )
    values_field = jnp.dot(
        values_field.reshape(batch_size * grid_points * grid_points // 2, 2 * grid_points),
        cas_paired,
        precision=solve_mode,
    )
    return values_field.reshape(batch_size, grid_points, grid_points, grid_points)


def cycle_term(own_block, visiting, cas_values, cas_paired, kernel):
    grid_points = kernel.shape[0]
    block_rows = own_block.shape[0]
    density = (own_block[:, None, :] * visiting[None, :, :]).reshape(
        block_rows * block_rows, grid_points, grid_points, grid_points
    )
    spectrum = transform(density, cas_values, cas_paired) * kernel[None]
    potential = transform(spectrum, cas_values, cas_paired).reshape(
        block_rows, block_rows, grid_points**3
    ) / float(grid_points**3)
    return jnp.sum(potential * visiting[None, :, :], axis=1)


def position_block(orbital_block, amount):
    bit_count = (lax.axis_size("blk") - 1).bit_length()
    for bit_level in range(bit_count):
        moved_block = passed_along(orbital_block, "blk", 1 << bit_level)
        orbital_block = jnp.where(amount // (1 << bit_level) % 2 == 1, moved_block, orbital_block)
    return orbital_block


def finish(accumulator, orbitals):
    replica = lax.axis_index("rep")
    exchanged = lax.psum_scatter(accumulator, "rep", scatter_dimension=1, tiled=True)
    quarter_cells = exchanged.shape[1]
    quarter = lax.dynamic_slice_in_dim(orbitals, replica * quarter_cells, quarter_cells, 1)
    slab_orbitals, slab_exchanged = (
        lax.all_to_all(quarter, "blk", split_axis=1, concat_axis=0, tiled=True),
        lax.all_to_all(exchanged, "blk", split_axis=1, concat_axis=0, tiled=True),
    )
    partial_value = lax.dot_general(
        slab_orbitals, slab_exchanged, (((1,), (1,)), ((), ())), precision=precise_mode
    ) / float(NG**3)
    gram_rows = lax.psum_scatter(partial_value, "blk", scatter_dimension=0, tiled=True)
    margin = lax.psum(gram_rows, "rep")
    return (exchanged, margin)


def local_steps(orbitals, offsets):
    cas_values = cas_table(NG)
    cas_paired = jnp.kron(jnp.eye(2, dtype=jnp.float32), cas_values)
    kernel = screened_kernel(NG)
    cycle_size = lax.axis_size("blk")
    replica = lax.axis_index("rep")
    start_block = offsets[replica]
    first_visit = position_block(orbitals, (start_block + 1) % cycle_size)
    behind = passed_along(first_visit, "blk", -1)
    accumulator = cycle_term(orbitals, first_visit, cas_values, cas_paired, kernel)
    ahead_block = passed_along(first_visit, "blk", 1)
    accumulator = accumulator + cycle_term(orbitals, ahead_block, cas_values, cas_paired, kernel)
    accumulator = accumulator + cycle_term(orbitals, behind, cas_values, cas_paired, kernel)
    return finish(accumulator, orbitals)


MESH = pl.DeviceIdType.MESH
LANES = 128


def two_halves(table):
    high = table.astype(jnp.bfloat16)
    low = (table - high.astype(np.float64)).astype(jnp.bfloat16)
    return high, low


def cas_tables(grid_points):
    index = np.arange(grid_points)
    angle = 2.0 * np.pi / grid_points * (np.outer(index, index) % grid_points)
    cas = np.cos(angle) + np.sin(angle)
    high, low = two_halves(np.kron(np.eye(2), cas))
    last_main = np.concatenate([high, high], axis=0)
    blocks = [cas[k::2, y::2] for k in range(2) for y in range(2)]
    y_high, y_low = two_halves(np.concatenate(blocks, axis=0))
    middle = np.concatenate([y_high, y_high, y_low], axis=1)
    x_high, x_low = two_halves(cas)
    first = np.concatenate([x_high, x_high, x_low], axis=1)
    return [jnp.asarray(t) for t in (last_main, low, middle, first)]


def split(values):
    high = values.astype(jnp.bfloat16)
    return high, (values - high.astype(jnp.float32)).astype(jnp.bfloat16)


def dot(a, b):
    return jnp.dot(a, b, preferred_element_type=jnp.float32)


def last_axis(values, main_ref, low_ref):
    high, low = split(values)
    return dot(jnp.concatenate([high, low], axis=1), main_ref[...]) + dot(high, low_ref[...])


def middle_axis(pair, middle_ref):
    half = pair.shape[0]
    high, low = split(pair)
    terms = dot(middle_ref[...], jnp.concatenate([high, low, high], axis=0))
    lane = lax.broadcasted_iota(jnp.int32, (half, pair.shape[1]), 1) % LANES
    first = lane < LANES // 2
    t = [terms[i * half : (i + 1) * half] for i in range(4)]
    straight = jnp.where(first, t[0], t[3])
    crossed = jnp.where(first, t[2], t[1])
    return [
        straight[:, at : at + LANES] + pltpu.roll(crossed[:, at : at + LANES], LANES // 2, 1)
        for at in (0, LANES)
    ]


def first_axis(values, first):
    high, low = split(values)
    return dot(first, jnp.concatenate([high, low, high], axis=0))


def chosen(index, values):
    found = jnp.int32(values[0])
    for at, value in enumerate(values):
        found = jnp.where(index == at, value, found)
    return found


EDGE_STEPS = (
    (0, (0, 0), None, None, 0),
    (0, (1, 0), (0, 0, 2), 0, 0),
    (4, (0, 1), None, None, 0),
    (6, (1, 1), None, None, 0),
    (7, None, (1, 0, 2), None, 0),
    (8, (0, 2), None, 1, 1),
    (8, (1, 2), (2, 0, 2), 2, 0),
)
INNER_STEPS = (
    (0, (0, 0), None, None, 0),
    (0, (1, 0), None, None, 0),
    (2, None, (0, 0, 2), None, 0),
    (4, None, None, 0, 0),
    (8, (0, 1), None, None, 0),
    (9, (0, 2), None, None, 0),
    (11, (1, 1), None, None, 0),
    (11, (1, 2), None, None, 0),
    (12, None, (1, 0, 2), 1, 0),
    (12, (0, 3), (2, 0, 2), 2, 1),
    (12, (1, 3), (3, 0, 2), 3, 0),
)
EDGE_ORDER = (0, 2, 3, 1)
INNER_ORDER = (1, 0, 2, 3)


def exchange_kernel(
    n,
    pieces,
    shared,
    offsets_hbm,
    psi_hbm,
    main_hbm,
    low_hbm,
    middle_hbm,
    first_hbm,
    exchanged_ref,
    margin_ref,
    orbs,
    fields,
    back_ref,
    pots,
    table,
    square,
    term_out,
    term_in,
    gram_out,
    gram_all,
    main_ref,
    low_ref,
    middle_ref,
    first_ref,
    offsets_ref,
    weights_ref,
    local_sem,
    up_sent,
    down_sent,
    over_sent,
    orb_got,
    rest_got,
    swap_sent,
    swap_got,
    term_sem,
    gram_sem,
):
    b = lax.axis_index("blk")
    r = lax.axis_index("rep")
    slab = orbs.shape[2]
    piece = slab // pieces
    plane = NG * NG // LANES
    slab_planes = slab // plane
    core = r % 2
    partner = r + 1 - 2 * core
    over = (r + 2) % n
    last = n - 1
    at_edge = (b == 0) | (b == last)
    edge = jnp.where(b < n // 2, 0, last)

    barrier = pltpu.get_barrier_semaphore()

    def greet(to):
        pl.semaphore_signal(barrier, inc=1, device_id=to, device_id_type=MESH)

    for j in range(1, n):
        greet({"rep": (r + j) % n})

    @pl.when(b > 0)
    def _():
        greet({"blk": b - 1})

    @pl.when(b < last)
    def _():
        greet({"blk": b + 1})

    def slab_rows(of):
        return pl.ds(pl.multiple_of(of * slab, slab), slab)

    local = [
        pltpu.make_async_copy(psi_hbm.at[slab_rows(r)], orbs.at[0, b], local_sem.at[0]),
        pltpu.make_async_copy(psi_hbm.at[slab_rows(over)], orbs.at[1, b], local_sem.at[1]),
        pltpu.make_async_copy(main_hbm, main_ref, local_sem.at[2]),
        pltpu.make_async_copy(low_hbm, low_ref, local_sem.at[3]),
        pltpu.make_async_copy(middle_hbm, middle_ref, local_sem.at[4]),
        pltpu.make_async_copy(first_hbm, first_ref, local_sem.at[5]),
        pltpu.make_async_copy(offsets_hbm, offsets_ref, local_sem.at[6]),
    ]
    for copy in local:
        copy.start()

    def folded(index):
        return jnp.where(index <= NG // 2, index, index - NG).astype(jnp.float32)

    lane = lax.broadcasted_iota(jnp.int32, (NG, LANES), 1)
    kx = folded(lax.broadcasted_iota(jnp.int32, (NG, LANES), 0))
    kz = folded(lane % NG)
    base = kx * kx + kz * kz

    def fill(k, _):
        ky = folded(2 * k + lane // NG)
        k_squared = base + ky * ky
        safe = jnp.maximum(k_squared, 1.0)
        scaled = screen_scale * safe / (4.0 * jnp.pi)
        screened = (1.0 - jnp.exp(-scaled)) / scaled
        here = pl.ds(pl.multiple_of(k * NG, NG), NG)
        table[here, :] = jnp.where(k_squared > 0.5, screened, 1.0)
        return 0


    def met(slot):
        low_side = jnp.where(at_edge, chosen(slot, EDGE_ORDER), chosen(slot, INNER_ORDER))
        return jnp.where(b < n // 2, low_side, last - low_side)

    def tick_of(t):
        near = 2 * pieces
        slot = jnp.where(at_edge, 1 + t // pieces, jnp.where(t < near, 2 - t % 2, 3))
        p = jnp.where(at_edge, t % pieces, jnp.where(t < near, t // 2, t - near))
        return slot, p

    def at_piece(p):
        return pl.ds(pl.multiple_of(p * piece, piece), piece)

    everything = pl.ds(0, slab)
    by_x = pl.ds(0, shared * piece)
    by_z = pl.ds(shared * piece, slab - shared * piece)

    def orb_copy(q_from, q_to, c, where, got, to, sent):
        return pltpu.make_async_remote_copy(
            src_ref=orbs.at[q_from, c, where],
            dst_ref=orbs.at[q_to, c, where],
            send_sem=sent,
            recv_sem=got,
            device_id=to,
            device_id_type=MESH,
        )

    def got_of(q, c, p):
        return orb_got.at[c, p] if q == 0 else rest_got.at[c]

    def up_copy(q, c, p, where):
        return orb_copy(q, q, c, where, got_of(q, c, p), {"blk": b + 1}, up_sent.at[q, c])

    def down_copy(q, c, p, where):
        return orb_copy(q, q, c, where, got_of(q, c, p), {"blk": b - 1}, down_sent.at[q, c])

    def over_copy(c, where):
        return orb_copy(0, 1, c, where, rest_got.at[c], {"rep": over}, over_sent.at[c])

    def goes_up(c):
        return (c <= b) & (b < last) & jnp.logical_not((c == b) & (b + 1 == last))

    def goes_down(c):
        return (c >= b) & (b > 0) & jnp.logical_not((c == b) & (b == 1))

    def halved(c):
        return ((c == 0) & (b == 1)) | ((c == last) & (b == last - 1))

    def comes(c):
        return (c != b) & jnp.logical_not(at_edge & (c == met(last)))

    def middle_all(planes):
        out = []
        for i in range(0, len(planes), 2):
            out += middle_axis(jnp.concatenate(planes[i : i + 2], axis=1), middle_ref)
        return jnp.concatenate(out, axis=0)

    def planes_of(values):
        return [values[i * plane : (i + 1) * plane] for i in range(slab_planes)]

    def forward(q, slot):
        c = met(slot)
        turned = last_axis(orbs[q, b] * orbs[q, c], main_ref, low_ref)
        fields[slot, slab_rows(jnp.where(q == 0, r, over)), :] = middle_all(planes_of(turned))

    def swap_copy(q, slot):
        here = slab_rows(jnp.where(q == 0, r, over))
        return pltpu.make_async_remote_copy(
            src_ref=fields.at[slot, here],
            dst_ref=fields.at[slot, here],
            send_sem=swap_sent.at[slot, q],
            recv_sem=swap_got.at[slot, q],
            device_id={"rep": partner},
            device_id_type=MESH,
        )

    def across(slot, part):
        wide = plane // 2
        start = part * wide

        @pl.when(part == 0)
        def _():
            for q in range(2):
                swap_copy(q, slot).wait_recv()
            square[...] = jnp.zeros_like(square)

        rows = first_ref[pl.ds(pl.multiple_of(r * slab_planes, 16), slab_planes), :]
        both = jnp.concatenate(
            [fields[slot, pl.ds(start + k, NG, stride=plane), :] for k in range(wide)], axis=1
        )
        factor = jnp.concatenate(
            [table[pl.ds(pl.multiple_of((start + k) * NG, NG), NG), :] for k in range(wide)], axis=1
        )
        spectrum = first_axis(both, first_ref[...])
        weighted = spectrum * factor
        folds = jnp.sum((spectrum * weighted).reshape(NG // 8, 8, wide * LANES), axis=0)
        total = square[...]
        for k in range(wide):
            total = total + folds[:, k * LANES : (k + 1) * LANES]
        square[...] = total
        back = first_axis(weighted, rows)
        for k in range(wide):
            places = pl.ds(start + k, slab_planes, stride=plane)
            back_ref[places, :] = back[:, k * LANES : (k + 1) * LANES]

    def weight_of(c, k):
        return weights_ref[(c - k + n) % n]

    def term_copy():
        return pltpu.make_async_remote_copy(
            src_ref=term_out,
            dst_ref=term_in,
            send_sem=term_sem.at[0],
            recv_sem=term_sem.at[1],
            device_id={"blk": edge},
            device_id_type=MESH,
        )

    def backward(slot):
        c = met(slot)
        scale = weight_of(b, c) / float(NG**3)
        potential = last_axis(middle_all(planes_of(back_ref[...])), main_ref, low_ref)
        pots[slot] = potential
        exchanged_ref[...] += potential * (orbs[0, c] * scale)

        @pl.when((slot == 1) & jnp.logical_not(at_edge))
        def _():
            there = weight_of(edge, b) / float(NG**3)
            term_out[...] = pots[1] * (orbs[0, b] * there)
            term_copy().start()

    row = lax.broadcasted_iota(jnp.int32, (n * n, LANES), 0)
    me = b * n + r

    def gram_copy(j, source):
        to = (me + j) % (n * n)
        return pltpu.make_async_remote_copy(
            src_ref=gram_out,
            dst_ref=gram_all.at[source],
            send_sem=gram_sem.at[0],
            recv_sem=gram_sem.at[1],
            device_id={"blk": to // n, "rep": to % n},
            device_id_type=MESH,
        )

    def every_gram():
        return pltpu.make_async_remote_copy(
            src_ref=gram_all.at[pl.ds(1, n * n - 1)],
            dst_ref=gram_all.at[pl.ds(1, n * n - 1)],
            send_sem=gram_sem.at[0],
            recv_sem=gram_sem.at[1],
            device_id={"rep": partner},
            device_id_type=MESH,
        )

    combos = [(i, j) for i in range(n - 1) for j in range(i, n)]

    def margin_terms():
        block = 32

        def one(t, sums):
            here = pl.ds(pl.multiple_of(t * block, block), block)
            met_orbs = [orbs[0, met(slot), here, :] for slot in range(n)]
            found = [pots[slot, here, :] for slot in range(n - 1)]
            own = [met_orbs[0] * v for v in met_orbs]
            theirs = [met_orbs[1] * v for v in met_orbs]
            terms = [found[i] * own[j] for i, j in combos] + [found[1] * v for v in theirs]
            return tuple(
                total + jnp.sum(term.reshape(block // 8, 8, LANES), axis=0)
                for total, term in zip(sums, terms)
            )

        zero = jnp.zeros((8, LANES), jnp.float32)
        sums = lax.fori_loop(0, slab // block, one, (zero,) * (len(combos) + n))
        packed = jnp.zeros((n * n, LANES), jnp.float32)

        def added(packed, line, wanted, a, c, k):
            spot = (row == a * n + c) & wanted
            return packed + jnp.where(spot, line * weight_of(c, k), 0.0)

        always = jnp.logical_not(at_edge)
        for at, (i, j) in enumerate(combos):
            wanted = always if i > 1 or j > 2 else jnp.bool_(True)
            line = jnp.sum(sums[at], axis=0, keepdims=True)
            a, c = met(i), met(j)
            packed = added(packed, line, wanted, a, c, b)
            if i != j:
                packed = added(packed, line, wanted, c, a, b)
            elif i == 1:
                packed = added(packed, line, at_edge, b, b, a)
        for j in range(n):
            line = jnp.sum(sums[len(combos) + j], axis=0, keepdims=True)
            a, k = met(j), met(1)
            packed = added(packed, line, always, a, b, k)
            if j != 0:
                packed = added(packed, line, always, b, a, k)
        gram_out[...] = packed
        for j in range(1, n * n):
            gram_copy(j, me).start()

    exchanged_ref[...] = jnp.zeros_like(exchanged_ref)
    for copy in local:
        copy.wait()

    @pl.when(at_edge)
    def _():
        pl.semaphore_wait(barrier, n)

    @pl.when(jnp.logical_not(at_edge))
    def _():
        pl.semaphore_wait(barrier, n + 1)

    def send_own(p, _):
        @pl.when(goes_up(b))
        def _():
            up_copy(0, b, p, at_piece(p)).start()

        @pl.when(goes_down(b))
        def _():
            down_copy(0, b, p, at_piece(p)).start()

        return 0

    lax.fori_loop(0, pieces, send_own, 0)

    @pl.when(b == 0)
    def _():
        up_copy(1, b, 0, by_z).start()

    @pl.when(b == last)
    def _():
        down_copy(1, b, 0, by_z).start()


    def receive(t, _):
        slot, p = tick_of(t)
        c = met(slot)
        up_copy(0, c, p, at_piece(p)).wait_recv()

        @pl.when(goes_up(c))
        def _():
            up_copy(0, c, p, at_piece(p)).start()

        @pl.when(goes_down(c))
        def _():
            down_copy(0, c, p, at_piece(p)).start()

        @pl.when(jnp.logical_not(halved(c)) | (p < shared))
        def _():
            over_copy(c, at_piece(p)).start()

        return 0

    def swapped(slot, _):
        for q in range(2):
            swap_copy(q, slot).wait_send()
        return 0

    def sent(c, _):
        @pl.when(goes_up(c))
        def _():
            up_copy(0, c, 0, everything).wait_send()

        @pl.when(goes_down(c))
        def _():
            down_copy(0, c, 0, everything).wait_send()

        @pl.when(comes(c) & halved(c))
        def _():
            over_copy(c, by_x).wait_send()

        @pl.when(comes(c) & jnp.logical_not(halved(c)))
        def _():
            over_copy(c, everything).wait_send()

        return 0

    def orbitals_sent():
        lax.fori_loop(0, jnp.where(at_edge, n - 2, last), swapped, 0)
        lax.fori_loop(0, n, sent, 0)

        @pl.when(b == 0)
        def _():
            up_copy(1, b, 0, by_z).wait_send()

        @pl.when(b == last)
        def _():
            down_copy(1, b, 0, by_z).wait_send()

    def planned(i, read):
        return jnp.where(
            at_edge,
            chosen(i, [read(step) for step in EDGE_STEPS]),
            chosen(i, [read(step) for step in INNER_STEPS]),
        )

    steps = jnp.where(at_edge, len(EDGE_STEPS), len(INNER_STEPS))

    def step(i, done):
        upto = planned(i, lambda step: step[0] * pieces // 4)
        lax.fori_loop(done, upto, receive, 0)
        q = planned(i, lambda step: step[1][0] if step[1] else -1)
        f_slot = planned(i, lambda step: step[1][1] if step[1] else 0)
        a_slot = planned(i, lambda step: step[2][0] if step[2] else 0)
        a_from = planned(i, lambda step: step[2][1] if step[2] else 0)
        a_to = planned(i, lambda step: step[2][2] if step[2] else 0)
        b_slot = planned(i, lambda step: -1 if step[3] is None else step[3])
        adds = planned(i, lambda step: step[4])

        @pl.when(i == steps - 1)
        def _():
            orbitals_sent()

        @pl.when((q == 1) & (f_slot > 0))
        def _():
            over_copy(met(f_slot), everything).wait_recv()

        @pl.when(q >= 0)
        def _():
            forward(q, f_slot)
            swap_copy(q, f_slot).start()

        @pl.when(i == 1)
        def _():
            lax.fori_loop(0, plane, fill, 0)
            for distance in range(n):
                found = jnp.float32(0.0)
                for replica in range(n):
                    for move in range(STEPS):
                        meets = (offsets_ref[replica] + move) % n == distance
                        found = found + jnp.where(meets, 1.0, 0.0)
                weights_ref[distance] = found

        def one_across(part, _):
            across(a_slot, part)
            return 0

        lax.fori_loop(a_from, a_to, one_across, 0)

        @pl.when(b_slot >= 0)
        def _():
            backward(b_slot)

        @pl.when(adds == 1)
        def _():
            margin_terms()

        return upto

    lax.fori_loop(0, steps, step, jnp.int32(0))

    for q in range(2):
        swap_copy(q, jnp.where(at_edge, n - 2, last)).wait_send()

    gram_all[me] = gram_out[...]
    every_gram().wait_recv()
    whole = gram_all[0]
    for k in range(1, n * n):
        whole = whole + gram_all[k]
    line = jnp.sum(square[...], axis=0, keepdims=True) * weight_of(b, met(2))
    whole = whole + jnp.where((row == b * n + b) & at_edge, line, 0.0)
    sums = jnp.sum(whole, axis=1, keepdims=True) / float(NG**6)
    at_row = lax.broadcasted_iota(jnp.int32, (n * n, n), 0)
    at_lane = lax.broadcasted_iota(jnp.int32, (n * n, n), 1)
    kept = jnp.where(at_row == b * n + at_lane, sums, 0.0)
    margin_ref[...] = jnp.sum(kept, axis=0, keepdims=True)

    @pl.when(at_edge)
    def _():
        term_copy().wait_recv()
        exchanged_ref[...] += term_in[...]

    @pl.when(jnp.logical_not(at_edge))
    def _():
        term_copy().wait_send()

    every_gram().wait_send()


def out_kernel(exchanged_ref, margin_ref, exchanged_out, margin_out, sems):
    copies = [
        pltpu.make_async_copy(exchanged_ref, exchanged_out, sems.at[0]),
        pltpu.make_async_copy(margin_ref, margin_out, sems.at[1]),
    ]
    for copy in copies:
        copy.start()
    for copy in copies:
        copy.wait()


def local_distances(orbitals, offsets):
    n = lax.axis_size("blk")
    pieces = 4
    shared = 1
    rows = orbitals.shape[1] // LANES
    slab = rows // n
    plane = NG * NG // LANES
    tables = cas_tables(NG)
    f32 = jnp.float32
    vmem = pl.BlockSpec(memory_space=pltpu.VMEM)
    dma = pltpu.SemaphoreType.DMA
    operands = [
        pltpu.with_memory_space_constraint(value, pltpu.HBM)
        for value in (offsets, orbitals.reshape(rows, LANES), *tables)
    ]
    exchanged, margin = pl.pallas_call(
        functools.partial(exchange_kernel, n, pieces, shared),
        out_shape=(
            jax.ShapeDtypeStruct((slab, LANES), f32),
            jax.ShapeDtypeStruct((1, n), f32),
        ),
        in_specs=[pl.BlockSpec(memory_space=pltpu.HBM)] * len(operands),
        out_specs=(vmem, vmem),
        scratch_shapes=[
            pltpu.VMEM((2, n, slab, LANES), f32),
            pltpu.VMEM((n, rows, LANES), f32),
            pltpu.VMEM((slab, LANES), f32),
            pltpu.VMEM((n, slab, LANES), f32),
            pltpu.VMEM((plane * NG, LANES), f32),
            pltpu.VMEM((8, LANES), f32),
            pltpu.VMEM((slab, LANES), f32),
            pltpu.VMEM((slab, LANES), f32),
            pltpu.VMEM((n * n, LANES), f32),
            pltpu.VMEM((n * n, n * n, LANES), f32),
            *[pltpu.VMEM(t.shape, t.dtype) for t in tables],
            pltpu.SMEM(offsets.shape, jnp.int32),
            pltpu.SMEM((n,), f32),
            dma((7,)),
            dma((2, n)),
            dma((2, n)),
            dma((n,)),
            dma((n, pieces)),
            dma((n,)),
            dma((n, 2)),
            dma((n, 2)),
            dma((2,)),
            dma((2,)),
        ],
        compiler_params=pltpu.CompilerParams(
            collective_id=0, has_side_effects=True, vmem_limit_bytes=32 << 20
        ),
    )(*operands)
    exchanged, margin = pl.pallas_call(
        out_kernel,
        out_shape=(
            jax.ShapeDtypeStruct((slab, LANES), f32),
            jax.ShapeDtypeStruct((1, n), f32),
        ),
        in_specs=[vmem, vmem],
        out_specs=(pl.BlockSpec(memory_space=pltpu.HBM),) * 2,
        scratch_shapes=[dma((2,))],
    )(*[pltpu.with_memory_space_constraint(value, pltpu.VMEM) for value in (exchanged, margin)])
    return exchanged.reshape(1, slab * LANES), margin


def solution(mesh):
    placed = (P(("groups", "blk"), None), P("groups"))
    paired = mesh.shape["blk"] == mesh.shape["rep"] == 4
    local = local_distances if paired else local_steps
    return jax.shard_map(
        local,
        mesh=mesh,
        in_specs=placed,
        out_specs=(P(("groups", "blk"), "rep"), P(("groups", "blk"), None)),
        check_vma=False,
    )
```

```python
import functools

import jax
import jax.numpy as jnp
import numpy as np
from jax import lax
from jax.experimental import pallas as pl
from jax.experimental.pallas import tpu as pltpu
from jax.sharding import PartitionSpec as P

NG = 64


precise_mode = lax.Precision.HIGHEST
solve_mode = lax.Precision.HIGH
STEPS = 3
screen_scale = 0.05


def passed_along(block, axis, distance):
    devices = range(lax.axis_size(axis))
    route = [((i - distance) % len(devices), i) for i in devices]
    return lax.ppermute(block, axis, route)


def cas_table(grid_points):
    grid_index = jnp.arange(grid_points, dtype=jnp.int32)
    product = grid_index[:, None] * grid_index[None, :] % grid_points
    phase_angle = 2.0 * jnp.pi / grid_points * product.astype(jnp.float32)
    return jnp.cos(phase_angle) + jnp.sin(phase_angle)


def screened_kernel(grid_points):
    grid_index = jnp.arange(grid_points, dtype=jnp.int32)
    folded = jnp.where(grid_index <= grid_points // 2, grid_index, grid_index - grid_points).astype(
        jnp.float32
    )
    squares = folded * folded
    k_squared = squares[:, None, None] + squares[None, :, None] + squares[None, None, :]
    safe_square = jnp.maximum(k_squared, 1.0)
    screened = (
        4.0
        * jnp.pi
        / (screen_scale * safe_square)
        * (1.0 - jnp.exp(-screen_scale * safe_square / (4.0 * jnp.pi)))
    )
    return jnp.where(k_squared > 0.5, screened, jnp.ones_like(screened))


def transform(values_field, cas_values, cas_paired):
    batch_size = values_field.shape[0]
    grid_points = values_field.shape[1]
    values_field = jnp.einsum(
        "kx,pxq->pkq",
        cas_values,
        values_field.reshape(batch_size, grid_points, grid_points * grid_points),
        precision=solve_mode,
    )
    values_field = jnp.einsum(
        "ky,ayz->akz",
        cas_values,
        values_field.reshape(batch_size * grid_points, grid_points, grid_points),
        precision=solve_mode,
    )
    values_field = jnp.dot(
        values_field.reshape(batch_size * grid_points * grid_points // 2, 2 * grid_points),
        cas_paired,
        precision=solve_mode,
    )
    return values_field.reshape(batch_size, grid_points, grid_points, grid_points)


def cycle_term(own_block, visiting, cas_values, cas_paired, kernel):
    grid_points = kernel.shape[0]
    block_rows = own_block.shape[0]
    density = (own_block[:, None, :] * visiting[None, :, :]).reshape(
        block_rows * block_rows, grid_points, grid_points, grid_points
    )
    spectrum = transform(density, cas_values, cas_paired) * kernel[None]
    potential = transform(spectrum, cas_values, cas_paired).reshape(
        block_rows, block_rows, grid_points**3
    ) / float(grid_points**3)
    return jnp.sum(potential * visiting[None, :, :], axis=1)


def position_block(orbital_block, amount):
    bit_count = (lax.axis_size("blk") - 1).bit_length()
    for bit_level in range(bit_count):
        moved_block = passed_along(orbital_block, "blk", 1 << bit_level)
        orbital_block = jnp.where(amount // (1 << bit_level) % 2 == 1, moved_block, orbital_block)
    return orbital_block


def finish(accumulator, orbitals):
    replica = lax.axis_index("rep")
    exchanged = lax.psum_scatter(accumulator, "rep", scatter_dimension=1, tiled=True)
    quarter_cells = exchanged.shape[1]
    quarter = lax.dynamic_slice_in_dim(orbitals, replica * quarter_cells, quarter_cells, 1)
    slab_orbitals, slab_exchanged = (
        lax.all_to_all(quarter, "blk", split_axis=1, concat_axis=0, tiled=True),
        lax.all_to_all(exchanged, "blk", split_axis=1, concat_axis=0, tiled=True),
    )
    partial_value = lax.dot_general(
        slab_orbitals, slab_exchanged, (((1,), (1,)), ((), ())), precision=precise_mode
    ) / float(NG**3)
    gram_rows = lax.psum_scatter(partial_value, "blk", scatter_dimension=0, tiled=True)
    margin = lax.psum(gram_rows, "rep")
    return (exchanged, margin)


def local_steps(orbitals, offsets):
    cas_values = cas_table(NG)
    cas_paired = jnp.kron(jnp.eye(2, dtype=jnp.float32), cas_values)
    kernel = screened_kernel(NG)
    cycle_size = lax.axis_size("blk")
    replica = lax.axis_index("rep")
    start_block = offsets[replica]
    first_visit = position_block(orbitals, (start_block + 1) % cycle_size)
    behind = passed_along(first_visit, "blk", -1)
    accumulator = cycle_term(orbitals, first_visit, cas_values, cas_paired, kernel)
    ahead_block = passed_along(first_visit, "blk", 1)
    accumulator = accumulator + cycle_term(orbitals, ahead_block, cas_values, cas_paired, kernel)
    accumulator = accumulator + cycle_term(orbitals, behind, cas_values, cas_paired, kernel)
    return finish(accumulator, orbitals)


MESH = pl.DeviceIdType.MESH
LANES = 128


def two_halves(table):
    high = table.astype(jnp.bfloat16)
    low = (table - high.astype(np.float64)).astype(jnp.bfloat16)
    return high, low


def cas_tables(grid_points):
    index = np.arange(grid_points)
    angle = 2.0 * np.pi / grid_points * (np.outer(index, index) % grid_points)
    cas = np.cos(angle) + np.sin(angle)
    high, low = two_halves(np.kron(np.eye(2), cas))
    zero = np.zeros_like(low)
    last_both = np.concatenate(
        [np.concatenate([high, low], axis=1), np.concatenate([high, zero], axis=1)], axis=0
    )
    blocks = [cas[k::2, y::2] for k in range(2) for y in range(2)]
    y_high, y_low = two_halves(np.concatenate(blocks, axis=0))
    middle = np.concatenate([y_high, y_high, y_low], axis=1)
    x_high, x_low = two_halves(cas)
    first = np.concatenate([x_high, x_high, x_low], axis=1)
    return [jnp.asarray(t) for t in (last_both, middle, first)]


def split(values):
    high = values.astype(jnp.bfloat16)
    return high, (values - high.astype(jnp.float32)).astype(jnp.bfloat16)


def dot(a, b):
    return jnp.dot(a, b, preferred_element_type=jnp.float32)


def last_axis(values, main_ref):
    high, low = split(values)
    terms = dot(jnp.concatenate([high, low], axis=1), main_ref[...])
    return terms[:, :LANES] + terms[:, LANES:]


def middle_axis(pair, middle_ref):
    half = pair.shape[0]
    high, low = split(pair)
    terms = dot(middle_ref[...], jnp.concatenate([high, low, high], axis=0))
    lane = lax.broadcasted_iota(jnp.int32, (half, pair.shape[1]), 1) % LANES
    first = lane < LANES // 2
    t = [terms[i * half : (i + 1) * half] for i in range(4)]
    straight = jnp.where(first, t[0], t[3])
    crossed = jnp.where(first, t[2], t[1])
    return [
        straight[:, at : at + LANES] + pltpu.roll(crossed[:, at : at + LANES], LANES // 2, 1)
        for at in (0, LANES)
    ]


def first_axis(values, first):
    high, low = split(values)
    return dot(first, jnp.concatenate([high, low, high], axis=0))


def chosen(index, values):
    found = jnp.int32(values[0])
    for at, value in enumerate(values):
        found = jnp.where(index == at, value, found)
    return found


EDGE_STEPS = (
    (0, (0, 0), None, None, 0),
    (0, (1, 0), (0, 0, 2), 0, 0),
    (4, (0, 1), None, None, 0),
    (6, (1, 1), None, None, 0),
    (7, None, (1, 0, 2), None, 0),
    (8, (0, 2), None, 1, 1),
    (8, (1, 2), (2, 0, 2), 2, 0),
)
INNER_STEPS = (
    (0, (0, 0), None, None, 0),
    (0, (1, 0), None, None, 0),
    (2, None, (0, 0, 2), None, 0),
    (4, None, None, 0, 0),
    (8, (0, 1), None, None, 0),
    (9, (0, 2), None, None, 0),
    (11, (1, 1), None, None, 0),
    (11, (1, 2), None, None, 0),
    (12, None, (1, 0, 2), 1, 0),
    (12, (0, 3), (2, 0, 2), 2, 1),
    (12, (1, 3), (3, 0, 2), 3, 0),
)
EDGE_ORDER = (0, 2, 3, 1)
INNER_ORDER = (1, 0, 2, 3)


def exchange_kernel(
    n,
    pieces,
    shared,
    offsets_hbm,
    psi_hbm,
    main_hbm,
    middle_hbm,
    first_hbm,
    exchanged_ref,
    margin_ref,
    orbs,
    fields,
    back_ref,
    pots,
    table,
    square,
    term_out,
    term_in,
    gram_out,
    gram_all,
    main_ref,
    middle_ref,
    first_ref,
    offsets_ref,
    weights_ref,
    local_sem,
    up_sent,
    down_sent,
    over_sent,
    orb_got,
    rest_got,
    swap_sent,
    swap_got,
    term_sem,
    gram_sem,
):
    b = lax.axis_index("blk")
    r = lax.axis_index("rep")
    slab = orbs.shape[2]
    piece = slab // pieces
    plane = NG * NG // LANES
    slab_planes = slab // plane
    core = r % 2
    partner = r + 1 - 2 * core
    over = (r + 2) % n
    last = n - 1
    at_edge = (b == 0) | (b == last)
    edge = jnp.where(b < n // 2, 0, last)

    barrier = pltpu.get_barrier_semaphore()

    def greet(to):
        pl.semaphore_signal(barrier, inc=1, device_id=to, device_id_type=MESH)

    for j in range(1, n):
        greet({"rep": (r + j) % n})

    @pl.when(b > 0)
    def _():
        greet({"blk": b - 1})

    @pl.when(b < last)
    def _():
        greet({"blk": b + 1})

    def slab_rows(of):
        return pl.ds(pl.multiple_of(of * slab, slab), slab)

    local = [
        pltpu.make_async_copy(psi_hbm.at[slab_rows(r)], orbs.at[0, b], local_sem.at[0]),
        pltpu.make_async_copy(psi_hbm.at[slab_rows(over)], orbs.at[1, b], local_sem.at[1]),
        pltpu.make_async_copy(main_hbm, main_ref, local_sem.at[2]),
        pltpu.make_async_copy(middle_hbm, middle_ref, local_sem.at[4]),
        pltpu.make_async_copy(first_hbm, first_ref, local_sem.at[5]),
        pltpu.make_async_copy(offsets_hbm, offsets_ref, local_sem.at[6]),
    ]
    for copy in local:
        copy.start()

    def folded(index):
        return jnp.where(index <= NG // 2, index, index - NG).astype(jnp.float32)

    lane = lax.broadcasted_iota(jnp.int32, (NG, LANES), 1)
    kx = folded(lax.broadcasted_iota(jnp.int32, (NG, LANES), 0))
    kz = folded(lane % NG)
    base = kx * kx + kz * kz

    def fill(k, _):
        ky = folded(2 * k + lane // NG)
        k_squared = base + ky * ky
        safe = jnp.maximum(k_squared, 1.0)
        scaled = screen_scale * safe / (4.0 * jnp.pi)
        screened = (1.0 - jnp.exp(-scaled)) / scaled
        here = pl.ds(pl.multiple_of(k * NG, NG), NG)
        table[here, :] = jnp.where(k_squared > 0.5, screened, 1.0)
        return 0


    def met(slot):
        low_side = jnp.where(at_edge, chosen(slot, EDGE_ORDER), chosen(slot, INNER_ORDER))
        return jnp.where(b < n // 2, low_side, last - low_side)

    def tick_of(t):
        near = 2 * pieces
        slot = jnp.where(at_edge, 1 + t // pieces, jnp.where(t < near, 2 - t % 2, 3))
        p = jnp.where(at_edge, t % pieces, jnp.where(t < near, t // 2, t - near))
        return slot, p

    def at_piece(p):
        return pl.ds(pl.multiple_of(p * piece, piece), piece)

    everything = pl.ds(0, slab)
    by_x = pl.ds(0, shared * piece)
    by_z = pl.ds(shared * piece, slab - shared * piece)

    def orb_copy(q_from, q_to, c, where, got, to, sent):
        return pltpu.make_async_remote_copy(
            src_ref=orbs.at[q_from, c, where],
            dst_ref=orbs.at[q_to, c, where],
            send_sem=sent,
            recv_sem=got,
            device_id=to,
            device_id_type=MESH,
        )

    def got_of(q, c, p):
        return orb_got.at[c, p] if q == 0 else rest_got.at[c]

    def up_copy(q, c, p, where):
        return orb_copy(q, q, c, where, got_of(q, c, p), {"blk": b + 1}, up_sent.at[q, c])

    def down_copy(q, c, p, where):
        return orb_copy(q, q, c, where, got_of(q, c, p), {"blk": b - 1}, down_sent.at[q, c])

    def over_copy(c, where):
        return orb_copy(0, 1, c, where, rest_got.at[c], {"rep": over}, over_sent.at[c])

    def goes_up(c):
        return (c <= b) & (b < last) & jnp.logical_not((c == b) & (b + 1 == last))

    def goes_down(c):
        return (c >= b) & (b > 0) & jnp.logical_not((c == b) & (b == 1))

    def halved(c):
        return ((c == 0) & (b == 1)) | ((c == last) & (b == last - 1))

    def comes(c):
        return (c != b) & jnp.logical_not(at_edge & (c == met(last)))

    def middle_all(planes):
        out = []
        for i in range(0, len(planes), 2):
            out += middle_axis(jnp.concatenate(planes[i : i + 2], axis=1), middle_ref)
        return jnp.concatenate(out, axis=0)

    def planes_of(values):
        return [values[i * plane : (i + 1) * plane] for i in range(slab_planes)]

    def forward(q, slot):
        c = met(slot)
        turned = last_axis(orbs[q, b] * orbs[q, c], main_ref)
        fields[slot, slab_rows(jnp.where(q == 0, r, over)), :] = middle_all(planes_of(turned))

    def swap_copy(q, slot):
        here = slab_rows(jnp.where(q == 0, r, over))
        return pltpu.make_async_remote_copy(
            src_ref=fields.at[slot, here],
            dst_ref=fields.at[slot, here],
            send_sem=swap_sent.at[slot, q],
            recv_sem=swap_got.at[slot, q],
            device_id={"rep": partner},
            device_id_type=MESH,
        )

    def across(slot, part):
        wide = plane // 2
        start = part * wide

        @pl.when(part == 0)
        def _():
            for q in range(2):
                swap_copy(q, slot).wait_recv()
            square[...] = jnp.zeros_like(square)

        rows = first_ref[pl.ds(pl.multiple_of(r * slab_planes, 16), slab_planes), :]
        both = jnp.concatenate(
            [fields[slot, pl.ds(start + k, NG, stride=plane), :] for k in range(wide)], axis=1
        )
        factor = jnp.concatenate(
            [table[pl.ds(pl.multiple_of((start + k) * NG, NG), NG), :] for k in range(wide)], axis=1
        )
        spectrum = first_axis(both, first_ref[...])
        weighted = spectrum * factor
        folds = jnp.sum((spectrum * weighted).reshape(NG // 8, 8, wide * LANES), axis=0)
        total = square[...]
        for k in range(wide):
            total = total + folds[:, k * LANES : (k + 1) * LANES]
        square[...] = total
        back = first_axis(weighted, rows)
        for k in range(wide):
            places = pl.ds(start + k, slab_planes, stride=plane)
            back_ref[places, :] = back[:, k * LANES : (k + 1) * LANES]

    def weight_of(c, k):
        return weights_ref[(c - k + n) % n]

    def term_copy():
        return pltpu.make_async_remote_copy(
            src_ref=term_out,
            dst_ref=term_in,
            send_sem=term_sem.at[0],
            recv_sem=term_sem.at[1],
            device_id={"blk": edge},
            device_id_type=MESH,
        )

    def backward(slot):
        c = met(slot)
        scale = weight_of(b, c) / float(NG**3)
        potential = last_axis(middle_all(planes_of(back_ref[...])), main_ref)
        pots[slot] = potential
        exchanged_ref[...] += potential * (orbs[0, c] * scale)

        @pl.when((slot == 1) & jnp.logical_not(at_edge))
        def _():
            there = weight_of(edge, b) / float(NG**3)
            term_out[...] = pots[1] * (orbs[0, b] * there)
            term_copy().start()

    row = lax.broadcasted_iota(jnp.int32, (n * n, LANES), 0)
    me = b * n + r

    def gram_copy(j, source):
        to = (me + j) % (n * n)
        return pltpu.make_async_remote_copy(
            src_ref=gram_out,
            dst_ref=gram_all.at[source],
            send_sem=gram_sem.at[0],
            recv_sem=gram_sem.at[1],
            device_id={"blk": to // n, "rep": to % n},
            device_id_type=MESH,
        )

    def every_gram():
        return pltpu.make_async_remote_copy(
            src_ref=gram_all.at[pl.ds(1, n * n - 1)],
            dst_ref=gram_all.at[pl.ds(1, n * n - 1)],
            send_sem=gram_sem.at[0],
            recv_sem=gram_sem.at[1],
            device_id={"rep": partner},
            device_id_type=MESH,
        )

    combos = [(i, j) for i in range(n - 1) for j in range(i, n)]

    def margin_terms():
        block = 32

        def one(t, sums):
            here = pl.ds(pl.multiple_of(t * block, block), block)
            met_orbs = [orbs[0, met(slot), here, :] for slot in range(n)]
            found = [pots[slot, here, :] for slot in range(n - 1)]
            own = [met_orbs[0] * v for v in met_orbs]
            theirs = [met_orbs[1] * v for v in met_orbs]
            terms = [found[i] * own[j] for i, j in combos] + [found[1] * v for v in theirs]
            return tuple(
                total + jnp.sum(term.reshape(block // 8, 8, LANES), axis=0)
                for total, term in zip(sums, terms)
            )

        zero = jnp.zeros((8, LANES), jnp.float32)
        sums = lax.fori_loop(0, slab // block, one, (zero,) * (len(combos) + n))
        packed = jnp.zeros((n * n, LANES), jnp.float32)

        def added(packed, line, wanted, a, c, k):
            spot = (row == a * n + c) & wanted
            return packed + jnp.where(spot, line * weight_of(c, k), 0.0)

        always = jnp.logical_not(at_edge)
        for at, (i, j) in enumerate(combos):
            wanted = always if i > 1 or j > 2 else jnp.bool_(True)
            line = jnp.sum(sums[at], axis=0, keepdims=True)
            a, c = met(i), met(j)
            packed = added(packed, line, wanted, a, c, b)
            if i != j:
                packed = added(packed, line, wanted, c, a, b)
            elif i == 1:
                packed = added(packed, line, at_edge, b, b, a)
        for j in range(n):
            line = jnp.sum(sums[len(combos) + j], axis=0, keepdims=True)
            a, k = met(j), met(1)
            packed = added(packed, line, always, a, b, k)
            if j != 0:
                packed = added(packed, line, always, b, a, k)
        gram_out[...] = packed
        for j in range(1, n * n):
            gram_copy(j, me).start()

    exchanged_ref[...] = jnp.zeros_like(exchanged_ref)
    for copy in local:
        copy.wait()

    @pl.when(at_edge)
    def _():
        pl.semaphore_wait(barrier, n)

    @pl.when(jnp.logical_not(at_edge))
    def _():
        pl.semaphore_wait(barrier, n + 1)

    def send_own(p, _):
        @pl.when(goes_up(b))
        def _():
            up_copy(0, b, p, at_piece(p)).start()

        @pl.when(goes_down(b))
        def _():
            down_copy(0, b, p, at_piece(p)).start()

        return 0

    lax.fori_loop(0, pieces, send_own, 0)

    @pl.when(b == 0)
    def _():
        up_copy(1, b, 0, by_z).start()

    @pl.when(b == last)
    def _():
        down_copy(1, b, 0, by_z).start()


    def receive(t, _):
        slot, p = tick_of(t)
        c = met(slot)
        up_copy(0, c, p, at_piece(p)).wait_recv()

        @pl.when(goes_up(c))
        def _():
            up_copy(0, c, p, at_piece(p)).start()

        @pl.when(goes_down(c))
        def _():
            down_copy(0, c, p, at_piece(p)).start()

        @pl.when(jnp.logical_not(halved(c)) | (p < shared))
        def _():
            over_copy(c, at_piece(p)).start()

        return 0

    def swapped(slot, _):
        for q in range(2):
            swap_copy(q, slot).wait_send()
        return 0

    def sent(c, _):
        @pl.when(goes_up(c))
        def _():
            up_copy(0, c, 0, everything).wait_send()

        @pl.when(goes_down(c))
        def _():
            down_copy(0, c, 0, everything).wait_send()

        @pl.when(comes(c) & halved(c))
        def _():
            over_copy(c, by_x).wait_send()

        @pl.when(comes(c) & jnp.logical_not(halved(c)))
        def _():
            over_copy(c, everything).wait_send()

        return 0

    def orbitals_sent():
        lax.fori_loop(0, jnp.where(at_edge, n - 2, last), swapped, 0)
        lax.fori_loop(0, n, sent, 0)

        @pl.when(b == 0)
        def _():
            up_copy(1, b, 0, by_z).wait_send()

        @pl.when(b == last)
        def _():
            down_copy(1, b, 0, by_z).wait_send()

    def packed_step(step):
        upto, ahead, over_x, home, adds = step
        code = upto
        code = code * 4 + (ahead[0] + 1 if ahead else 0)
        code = code * 4 + (ahead[1] if ahead else 0)
        code = code * 8 + (over_x[0] + 1 if over_x else 0)
        code = code * 8 + (0 if home is None else home + 1)
        return code * 2 + adds

    steps = jnp.where(at_edge, len(EDGE_STEPS), len(INNER_STEPS))

    def step(i, done):
        code = jnp.where(
            at_edge,
            chosen(i, [packed_step(step) for step in EDGE_STEPS]),
            chosen(i, [packed_step(step) for step in INNER_STEPS]),
        )
        adds = code % 2
        b_slot = code // 2 % 8 - 1
        a_slot = code // 16 % 8 - 1
        f_slot = code // 128 % 4
        q = code // 512 % 4 - 1
        upto = code // 2048 * pieces // 4
        lax.fori_loop(done, upto, receive, 0)

        @pl.when((q == 1) & (f_slot > 0))
        def _():
            over_copy(met(f_slot), everything).wait_recv()

        @pl.when(q >= 0)
        def _():
            forward(q, f_slot)
            swap_copy(q, f_slot).start()

        @pl.when(i == 1)
        def _():
            lax.fori_loop(0, plane, fill, 0)
            for distance in range(n):
                found = jnp.float32(0.0)
                for replica in range(n):
                    for move in range(STEPS):
                        meets = (offsets_ref[replica] + move) % n == distance
                        found = found + jnp.where(meets, 1.0, 0.0)
                weights_ref[distance] = found

        def one_across(part, _):
            across(a_slot, part)
            return 0

        lax.fori_loop(0, jnp.where(a_slot >= 0, 2, 0), one_across, 0)

        @pl.when(b_slot >= 0)
        def _():
            backward(b_slot)

        @pl.when(adds == 1)
        def _():
            margin_terms()

        return upto

    lax.fori_loop(0, steps, step, jnp.int32(0))

    for q in range(2):
        swap_copy(q, jnp.where(at_edge, n - 2, last)).wait_send()

    orbitals_sent()
    gram_all[me] = gram_out[...]
    every_gram().wait_recv()
    whole = gram_all[0]
    for k in range(1, n * n):
        whole = whole + gram_all[k]
    line = jnp.sum(square[...], axis=0, keepdims=True) * weight_of(b, met(2))
    whole = whole + jnp.where((row == b * n + b) & at_edge, line, 0.0)
    sums = jnp.sum(whole, axis=1, keepdims=True) / float(NG**6)
    at_row = lax.broadcasted_iota(jnp.int32, (n * n, n), 0)
    at_lane = lax.broadcasted_iota(jnp.int32, (n * n, n), 1)
    kept = jnp.where(at_row == b * n + at_lane, sums, 0.0)
    margin_ref[...] = jnp.sum(kept, axis=0, keepdims=True)

    @pl.when(at_edge)
    def _():
        term_copy().wait_recv()
        exchanged_ref[...] += term_in[...]

    @pl.when(jnp.logical_not(at_edge))
    def _():
        term_copy().wait_send()

    every_gram().wait_send()


def out_kernel(exchanged_ref, margin_ref, exchanged_out, margin_out, sems):
    copies = [
        pltpu.make_async_copy(exchanged_ref, exchanged_out, sems.at[0]),
        pltpu.make_async_copy(margin_ref, margin_out, sems.at[1]),
    ]
    for copy in copies:
        copy.start()
    for copy in copies:
        copy.wait()


def local_distances(orbitals, offsets):
    n = lax.axis_size("blk")
    pieces = 4
    shared = 1
    rows = orbitals.shape[1] // LANES
    slab = rows // n
    plane = NG * NG // LANES
    tables = cas_tables(NG)
    f32 = jnp.float32
    vmem = pl.BlockSpec(memory_space=pltpu.VMEM)
    dma = pltpu.SemaphoreType.DMA
    operands = [
        pltpu.with_memory_space_constraint(value, pltpu.HBM)
        for value in (offsets, orbitals.reshape(rows, LANES), *tables)
    ]
    exchanged, margin = pl.pallas_call(
        functools.partial(exchange_kernel, n, pieces, shared),
        out_shape=(
            jax.ShapeDtypeStruct((slab, LANES), f32),
            jax.ShapeDtypeStruct((1, n), f32),
        ),
        in_specs=[pl.BlockSpec(memory_space=pltpu.HBM)] * len(operands),
        out_specs=(vmem, vmem),
        scratch_shapes=[
            pltpu.VMEM((2, n, slab, LANES), f32),
            pltpu.VMEM((n, rows, LANES), f32),
            pltpu.VMEM((slab, LANES), f32),
            pltpu.VMEM((n, slab, LANES), f32),
            pltpu.VMEM((plane * NG, LANES), f32),
            pltpu.VMEM((8, LANES), f32),
            pltpu.VMEM((slab, LANES), f32),
            pltpu.VMEM((slab, LANES), f32),
            pltpu.VMEM((n * n, LANES), f32),
            pltpu.VMEM((n * n, n * n, LANES), f32),
            *[pltpu.VMEM(t.shape, t.dtype) for t in tables],
            pltpu.SMEM(offsets.shape, jnp.int32),
            pltpu.SMEM((n,), f32),
            dma((7,)),
            dma((2, n)),
            dma((2, n)),
            dma((n,)),
            dma((n, pieces)),
            dma((n,)),
            dma((n, 2)),
            dma((n, 2)),
            dma((2,)),
            dma((2,)),
        ],
        compiler_params=pltpu.CompilerParams(
            collective_id=0, has_side_effects=True, vmem_limit_bytes=32 << 20
        ),
    )(*operands)
    exchanged, margin = pl.pallas_call(
        out_kernel,
        out_shape=(
            jax.ShapeDtypeStruct((slab, LANES), f32),
            jax.ShapeDtypeStruct((1, n), f32),
        ),
        in_specs=[vmem, vmem],
        out_specs=(pl.BlockSpec(memory_space=pltpu.HBM),) * 2,
        scratch_shapes=[dma((2,))],
    )(*[pltpu.with_memory_space_constraint(value, pltpu.VMEM) for value in (exchanged, margin)])
    return exchanged.reshape(1, slab * LANES), margin


def solution(mesh):
    placed = (P(("groups", "blk"), None), P("groups"))
    paired = mesh.shape["blk"] == mesh.shape["rep"] == 4
    local = local_distances if paired else local_steps
    return jax.shard_map(
        local,
        mesh=mesh,
        in_specs=placed,
        out_specs=(P(("groups", "blk"), "rep"), P(("groups", "blk"), None)),
        check_vma=False,
    )
```

```python
import functools

import jax
import jax.numpy as jnp
import numpy as np
from jax import lax
from jax.experimental import pallas as pl
from jax.experimental.pallas import tpu as pltpu
from jax.sharding import PartitionSpec as P

NG = 64


precise_mode = lax.Precision.HIGHEST
solve_mode = lax.Precision.HIGH
STEPS = 3
screen_scale = 0.05


def passed_along(block, axis, distance):
    devices = range(lax.axis_size(axis))
    route = [((i - distance) % len(devices), i) for i in devices]
    return lax.ppermute(block, axis, route)


def cas_table(grid_points):
    grid_index = jnp.arange(grid_points, dtype=jnp.int32)
    product = grid_index[:, None] * grid_index[None, :] % grid_points
    phase_angle = 2.0 * jnp.pi / grid_points * product.astype(jnp.float32)
    return jnp.cos(phase_angle) + jnp.sin(phase_angle)


def screened_kernel(grid_points):
    grid_index = jnp.arange(grid_points, dtype=jnp.int32)
    folded = jnp.where(grid_index <= grid_points // 2, grid_index, grid_index - grid_points).astype(
        jnp.float32
    )
    squares = folded * folded
    k_squared = squares[:, None, None] + squares[None, :, None] + squares[None, None, :]
    safe_square = jnp.maximum(k_squared, 1.0)
    screened = (
        4.0
        * jnp.pi
        / (screen_scale * safe_square)
        * (1.0 - jnp.exp(-screen_scale * safe_square / (4.0 * jnp.pi)))
    )
    return jnp.where(k_squared > 0.5, screened, jnp.ones_like(screened))


def transform(values_field, cas_values, cas_paired):
    batch_size = values_field.shape[0]
    grid_points = values_field.shape[1]
    values_field = jnp.einsum(
        "kx,pxq->pkq",
        cas_values,
        values_field.reshape(batch_size, grid_points, grid_points * grid_points),
        precision=solve_mode,
    )
    values_field = jnp.einsum(
        "ky,ayz->akz",
        cas_values,
        values_field.reshape(batch_size * grid_points, grid_points, grid_points),
        precision=solve_mode,
    )
    values_field = jnp.dot(
        values_field.reshape(batch_size * grid_points * grid_points // 2, 2 * grid_points),
        cas_paired,
        precision=solve_mode,
    )
    return values_field.reshape(batch_size, grid_points, grid_points, grid_points)


def cycle_term(own_block, visiting, cas_values, cas_paired, kernel):
    grid_points = kernel.shape[0]
    block_rows = own_block.shape[0]
    density = (own_block[:, None, :] * visiting[None, :, :]).reshape(
        block_rows * block_rows, grid_points, grid_points, grid_points
    )
    spectrum = transform(density, cas_values, cas_paired) * kernel[None]
    potential = transform(spectrum, cas_values, cas_paired).reshape(
        block_rows, block_rows, grid_points**3
    ) / float(grid_points**3)
    return jnp.sum(potential * visiting[None, :, :], axis=1)


def position_block(orbital_block, amount):
    bit_count = (lax.axis_size("blk") - 1).bit_length()
    for bit_level in range(bit_count):
        moved_block = passed_along(orbital_block, "blk", 1 << bit_level)
        orbital_block = jnp.where(amount // (1 << bit_level) % 2 == 1, moved_block, orbital_block)
    return orbital_block


def finish(accumulator, orbitals):
    replica = lax.axis_index("rep")
    exchanged = lax.psum_scatter(accumulator, "rep", scatter_dimension=1, tiled=True)
    quarter_cells = exchanged.shape[1]
    quarter = lax.dynamic_slice_in_dim(orbitals, replica * quarter_cells, quarter_cells, 1)
    slab_orbitals, slab_exchanged = (
        lax.all_to_all(quarter, "blk", split_axis=1, concat_axis=0, tiled=True),
        lax.all_to_all(exchanged, "blk", split_axis=1, concat_axis=0, tiled=True),
    )
    partial_value = lax.dot_general(
        slab_orbitals, slab_exchanged, (((1,), (1,)), ((), ())), precision=precise_mode
    ) / float(NG**3)
    gram_rows = lax.psum_scatter(partial_value, "blk", scatter_dimension=0, tiled=True)
    margin = lax.psum(gram_rows, "rep")
    return (exchanged, margin)


def local_steps(orbitals, offsets):
    cas_values = cas_table(NG)
    cas_paired = jnp.kron(jnp.eye(2, dtype=jnp.float32), cas_values)
    kernel = screened_kernel(NG)
    cycle_size = lax.axis_size("blk")
    replica = lax.axis_index("rep")
    start_block = offsets[replica]
    first_visit = position_block(orbitals, (start_block + 1) % cycle_size)
    behind = passed_along(first_visit, "blk", -1)
    accumulator = cycle_term(orbitals, first_visit, cas_values, cas_paired, kernel)
    ahead_block = passed_along(first_visit, "blk", 1)
    accumulator = accumulator + cycle_term(orbitals, ahead_block, cas_values, cas_paired, kernel)
    accumulator = accumulator + cycle_term(orbitals, behind, cas_values, cas_paired, kernel)
    return finish(accumulator, orbitals)


MESH = pl.DeviceIdType.MESH
LANES = 128


def two_halves(table):
    high = table.astype(jnp.bfloat16)
    low = (table - high.astype(np.float64)).astype(jnp.bfloat16)
    return high, low


def cas_tables(grid_points):
    index = np.arange(grid_points)
    angle = 2.0 * np.pi / grid_points * (np.outer(index, index) % grid_points)
    cas = np.cos(angle) + np.sin(angle)
    high, low = two_halves(np.kron(np.eye(2), cas))
    zero = np.zeros_like(low)
    last_both = np.concatenate(
        [np.concatenate([high, low], axis=1), np.concatenate([high, zero], axis=1)], axis=0
    )
    blocks = [cas[k::2, y::2] for k in range(2) for y in range(2)]
    y_high, y_low = two_halves(np.concatenate(blocks, axis=0))
    middle = np.concatenate([y_high, y_high, y_low], axis=1)
    x_high, x_low = two_halves(cas)
    first = np.concatenate([x_high, x_high, x_low], axis=1)
    return [jnp.asarray(t) for t in (last_both, middle, first)]


def split(values):
    high = values.astype(jnp.bfloat16)
    return high, (values - high.astype(jnp.float32)).astype(jnp.bfloat16)


def dot(a, b):
    return jnp.dot(a, b, preferred_element_type=jnp.float32)


def last_axis(values, main_ref):
    high, low = split(values)
    terms = dot(jnp.concatenate([high, low], axis=1), main_ref[...])
    return terms[:, :LANES] + terms[:, LANES:]


def middle_axis(pair, middle_ref):
    half = pair.shape[0]
    high, low = split(pair)
    terms = dot(middle_ref[...], jnp.concatenate([high, low, high], axis=0))
    lane = lax.broadcasted_iota(jnp.int32, (half, pair.shape[1]), 1) % LANES
    first = lane < LANES // 2
    t = [terms[i * half : (i + 1) * half] for i in range(4)]
    straight = jnp.where(first, t[0], t[3])
    crossed = jnp.where(first, t[2], t[1])
    return [
        straight[:, at : at + LANES] + pltpu.roll(crossed[:, at : at + LANES], LANES // 2, 1)
        for at in (0, LANES)
    ]


def first_axis(values, first):
    high, low = split(values)
    return dot(first, jnp.concatenate([high, low, high], axis=0))


def chosen(index, values):
    found = jnp.int32(values[0])
    for at, value in enumerate(values):
        found = jnp.where(index == at, value, found)
    return found


EDGE_STEPS = (
    (0, (0, 0), None, None, 0),
    (0, (1, 0), (0, 0, 2), 0, 0),
    (4, (0, 1), None, None, 0),
    (6, (1, 1), None, None, 0),
    (7, None, (1, 0, 2), None, 0),
    (8, (0, 2), None, 1, 1),
    (8, (1, 2), (2, 0, 2), 2, 0),
)
INNER_STEPS = (
    (0, (0, 0), None, None, 0),
    (0, (1, 0), None, None, 0),
    (2, None, (0, 0, 2), None, 0),
    (4, None, None, 0, 0),
    (8, (0, 1), None, None, 0),
    (9, (0, 2), None, None, 0),
    (11, (1, 1), None, None, 0),
    (11, (1, 2), None, None, 0),
    (12, None, (1, 0, 2), 1, 0),
    (12, (0, 3), (2, 0, 2), 2, 1),
    (12, (1, 3), (3, 0, 2), 3, 0),
)
EDGE_ORDER = (0, 2, 3, 1)
INNER_ORDER = (1, 0, 2, 3)


def exchange_kernel(
    n,
    pieces,
    shared,
    offsets_hbm,
    psi_hbm,
    main_hbm,
    middle_hbm,
    first_hbm,
    exchanged_ref,
    margin_ref,
    orbs,
    fields,
    back_ref,
    pots,
    table,
    square,
    term_out,
    term_in,
    gram_out,
    gram_all,
    main_ref,
    middle_ref,
    first_ref,
    offsets_ref,
    weights_ref,
    local_sem,
    up_sent,
    down_sent,
    over_sent,
    orb_got,
    rest_got,
    swap_sent,
    swap_got,
    term_sem,
    gram_sem,
):
    b = lax.axis_index("blk")
    r = lax.axis_index("rep")
    slab = orbs.shape[2]
    piece = slab // pieces
    plane = NG * NG // LANES
    slab_planes = slab // plane
    core = r % 2
    partner = r + 1 - 2 * core
    over = (r + 2) % n
    last = n - 1
    at_edge = (b == 0) | (b == last)
    edge = jnp.where(b < n // 2, 0, last)

    barrier = pltpu.get_barrier_semaphore()

    def greet(to):
        pl.semaphore_signal(barrier, inc=1, device_id=to, device_id_type=MESH)

    for j in range(1, n):
        greet({"rep": (r + j) % n})

    @pl.when(b > 0)
    def _():
        greet({"blk": b - 1})

    @pl.when(b < last)
    def _():
        greet({"blk": b + 1})

    def slab_rows(of):
        return pl.ds(pl.multiple_of(of * slab, slab), slab)

    local = [
        pltpu.make_async_copy(psi_hbm.at[slab_rows(r)], orbs.at[0, b], local_sem.at[0]),
        pltpu.make_async_copy(psi_hbm.at[slab_rows(over)], orbs.at[1, b], local_sem.at[1]),
        pltpu.make_async_copy(main_hbm, main_ref, local_sem.at[2]),
        pltpu.make_async_copy(middle_hbm, middle_ref, local_sem.at[4]),
        pltpu.make_async_copy(first_hbm, first_ref, local_sem.at[5]),
        pltpu.make_async_copy(offsets_hbm, offsets_ref, local_sem.at[6]),
    ]
    for copy in local:
        copy.start()

    def folded(index):
        return jnp.where(index <= NG // 2, index, index - NG).astype(jnp.float32)

    lane = lax.broadcasted_iota(jnp.int32, (NG, LANES), 1)
    kx = folded(lax.broadcasted_iota(jnp.int32, (NG, LANES), 0))
    kz = folded(lane % NG)
    base = kx * kx + kz * kz

    def fill(k, _):
        ky = folded(2 * k + lane // NG)
        k_squared = base + ky * ky
        safe = jnp.maximum(k_squared, 1.0)
        scaled = screen_scale * safe / (4.0 * jnp.pi)
        screened = (1.0 - jnp.exp(-scaled)) / scaled
        here = pl.ds(pl.multiple_of(k * NG, NG), NG)
        table[here, :] = jnp.where(k_squared > 0.5, screened, 1.0)
        return 0


    def met(slot):
        low_side = jnp.where(at_edge, chosen(slot, EDGE_ORDER), chosen(slot, INNER_ORDER))
        return jnp.where(b < n // 2, low_side, last - low_side)

    def tick_of(t):
        near = 2 * pieces
        slot = jnp.where(at_edge, 1 + t // pieces, jnp.where(t < near, 2 - t % 2, 3))
        p = jnp.where(at_edge, t % pieces, jnp.where(t < near, t // 2, t - near))
        return slot, p

    def at_piece(p):
        return pl.ds(pl.multiple_of(p * piece, piece), piece)

    everything = pl.ds(0, slab)
    by_x = pl.ds(0, shared * piece)
    by_z = pl.ds(shared * piece, slab - shared * piece)

    def orb_copy(q_from, q_to, c, where, got, to, sent):
        return pltpu.make_async_remote_copy(
            src_ref=orbs.at[q_from, c, where],
            dst_ref=orbs.at[q_to, c, where],
            send_sem=sent,
            recv_sem=got,
            device_id=to,
            device_id_type=MESH,
        )

    def got_of(q, c, p):
        return orb_got.at[c, p] if q == 0 else rest_got.at[c]

    def up_copy(q, c, p, where):
        return orb_copy(q, q, c, where, got_of(q, c, p), {"blk": b + 1}, up_sent.at[q, c])

    def down_copy(q, c, p, where):
        return orb_copy(q, q, c, where, got_of(q, c, p), {"blk": b - 1}, down_sent.at[q, c])

    def over_copy(c, where):
        return orb_copy(0, 1, c, where, rest_got.at[c], {"rep": over}, over_sent.at[c])

    def goes_up(c):
        return (c <= b) & (b < last) & jnp.logical_not((c == b) & (b + 1 == last))

    def goes_down(c):
        return (c >= b) & (b > 0) & jnp.logical_not((c == b) & (b == 1))

    def halved(c):
        return ((c == 0) & (b == 1)) | ((c == last) & (b == last - 1))

    def comes(c):
        return (c != b) & jnp.logical_not(at_edge & (c == met(last)))

    def middle_all(planes):
        out = []
        for i in range(0, len(planes), 2):
            out += middle_axis(jnp.concatenate(planes[i : i + 2], axis=1), middle_ref)
        return jnp.concatenate(out, axis=0)

    def planes_of(values):
        return [values[i * plane : (i + 1) * plane] for i in range(slab_planes)]

    def forward(q, slot):
        c = met(slot)
        turned = last_axis(orbs[q, b] * orbs[q, c], main_ref)
        fields[slot, slab_rows(jnp.where(q == 0, r, over)), :] = middle_all(planes_of(turned))

    def swap_copy(q, slot):
        here = slab_rows(jnp.where(q == 0, r, over))
        return pltpu.make_async_remote_copy(
            src_ref=fields.at[slot, here],
            dst_ref=fields.at[slot, here],
            send_sem=swap_sent.at[slot, q],
            recv_sem=swap_got.at[slot, q],
            device_id={"rep": partner},
            device_id_type=MESH,
        )

    def across(slot, part):
        wide = plane // 2
        start = part * wide

        @pl.when(part == 0)
        def _():
            for q in range(2):
                swap_copy(q, slot).wait_recv()
            square[...] = jnp.zeros_like(square)

        rows = first_ref[pl.ds(pl.multiple_of(r * slab_planes, 16), slab_planes), :]
        both = jnp.concatenate(
            [fields[slot, pl.ds(start + k, NG, stride=plane), :] for k in range(wide)], axis=1
        )
        factor = jnp.concatenate(
            [table[pl.ds(pl.multiple_of((start + k) * NG, NG), NG), :] for k in range(wide)], axis=1
        )
        spectrum = first_axis(both, first_ref[...])
        weighted = spectrum * factor
        folds = jnp.sum((spectrum * weighted).reshape(NG // 8, 8, wide * LANES), axis=0)
        total = square[...]
        for k in range(wide):
            total = total + folds[:, k * LANES : (k + 1) * LANES]
        square[...] = total
        back = first_axis(weighted, rows)
        for k in range(wide):
            places = pl.ds(start + k, slab_planes, stride=plane)
            back_ref[places, :] = back[:, k * LANES : (k + 1) * LANES]

    def weight_of(c, k):
        return weights_ref[(c - k + n) % n]

    def term_copy():
        return pltpu.make_async_remote_copy(
            src_ref=term_out,
            dst_ref=term_in,
            send_sem=term_sem.at[0],
            recv_sem=term_sem.at[1],
            device_id={"blk": edge},
            device_id_type=MESH,
        )

    def backward(slot):
        c = met(slot)
        scale = weight_of(b, c) / float(NG**3)
        potential = last_axis(middle_all(planes_of(back_ref[...])), main_ref)
        pots[slot] = potential
        exchanged_ref[...] += potential * (orbs[0, c] * scale)

        @pl.when((slot == 1) & jnp.logical_not(at_edge))
        def _():
            there = weight_of(edge, b) / float(NG**3)
            term_out[...] = pots[1] * (orbs[0, b] * there)
            term_copy().start()

    row = lax.broadcasted_iota(jnp.int32, (n * n, LANES), 0)
    me = b * n + r

    def gram_copy(j, source):
        to = (me + j) % (n * n)
        return pltpu.make_async_remote_copy(
            src_ref=gram_out,
            dst_ref=gram_all.at[source],
            send_sem=gram_sem.at[0],
            recv_sem=gram_sem.at[1],
            device_id={"blk": to // n, "rep": to % n},
            device_id_type=MESH,
        )

    def every_gram():
        return pltpu.make_async_remote_copy(
            src_ref=gram_all.at[pl.ds(1, n * n - 1)],
            dst_ref=gram_all.at[pl.ds(1, n * n - 1)],
            send_sem=gram_sem.at[0],
            recv_sem=gram_sem.at[1],
            device_id={"rep": partner},
            device_id_type=MESH,
        )

    combos = [(i, j) for i in range(n - 1) for j in range(i, n)]

    def margin_terms():
        block = 128

        def one(t, sums):
            here = pl.ds(pl.multiple_of(t * block, block), block)
            met_orbs = [orbs[0, met(slot), here, :] for slot in range(n)]
            found = [pots[slot, here, :] for slot in range(n - 1)]
            own = [met_orbs[0] * v for v in met_orbs]
            theirs = [met_orbs[1] * v for v in met_orbs]
            terms = [found[i] * own[j] for i, j in combos] + [found[1] * v for v in theirs]
            return tuple(
                total + jnp.sum(term.reshape(block // 8, 8, LANES), axis=0)
                for total, term in zip(sums, terms)
            )

        zero = jnp.zeros((8, LANES), jnp.float32)
        sums = lax.fori_loop(0, slab // block, one, (zero,) * (len(combos) + n))
        packed = jnp.zeros((n * n, LANES), jnp.float32)

        def added(packed, line, wanted, a, c, k):
            spot = (row == a * n + c) & wanted
            return packed + jnp.where(spot, line * weight_of(c, k), 0.0)

        always = jnp.logical_not(at_edge)
        for at, (i, j) in enumerate(combos):
            wanted = always if i > 1 or j > 2 else jnp.bool_(True)
            line = jnp.sum(sums[at], axis=0, keepdims=True)
            a, c = met(i), met(j)
            packed = added(packed, line, wanted, a, c, b)
            if i != j:
                packed = added(packed, line, wanted, c, a, b)
            elif i == 1:
                packed = added(packed, line, at_edge, b, b, a)
        for j in range(n):
            line = jnp.sum(sums[len(combos) + j], axis=0, keepdims=True)
            a, k = met(j), met(1)
            packed = added(packed, line, always, a, b, k)
            if j != 0:
                packed = added(packed, line, always, b, a, k)
        gram_out[...] = packed
        for j in range(1, n * n):
            gram_copy(j, me).start()

    exchanged_ref[...] = jnp.zeros_like(exchanged_ref)
    for copy in local:
        copy.wait()

    @pl.when(at_edge)
    def _():
        pl.semaphore_wait(barrier, n)

    @pl.when(jnp.logical_not(at_edge))
    def _():
        pl.semaphore_wait(barrier, n + 1)

    def send_own(p, _):
        @pl.when(goes_up(b))
        def _():
            up_copy(0, b, p, at_piece(p)).start()

        @pl.when(goes_down(b))
        def _():
            down_copy(0, b, p, at_piece(p)).start()

        return 0

    lax.fori_loop(0, pieces, send_own, 0)

    @pl.when(b == 0)
    def _():
        up_copy(1, b, 0, by_z).start()

    @pl.when(b == last)
    def _():
        down_copy(1, b, 0, by_z).start()


    def receive(t, _):
        slot, p = tick_of(t)
        c = met(slot)
        up_copy(0, c, p, at_piece(p)).wait_recv()

        @pl.when(goes_up(c))
        def _():
            up_copy(0, c, p, at_piece(p)).start()

        @pl.when(goes_down(c))
        def _():
            down_copy(0, c, p, at_piece(p)).start()

        @pl.when(jnp.logical_not(halved(c)) | (p < shared))
        def _():
            over_copy(c, at_piece(p)).start()

        return 0

    def swapped(slot, _):
        for q in range(2):
            swap_copy(q, slot).wait_send()
        return 0

    def sent(c, _):
        @pl.when(goes_up(c))
        def _():
            up_copy(0, c, 0, everything).wait_send()

        @pl.when(goes_down(c))
        def _():
            down_copy(0, c, 0, everything).wait_send()

        @pl.when(comes(c) & halved(c))
        def _():
            over_copy(c, by_x).wait_send()

        @pl.when(comes(c) & jnp.logical_not(halved(c)))
        def _():
            over_copy(c, everything).wait_send()

        return 0

    def orbitals_sent():
        lax.fori_loop(0, jnp.where(at_edge, n - 2, last), swapped, 0)
        lax.fori_loop(0, n, sent, 0)

        @pl.when(b == 0)
        def _():
            up_copy(1, b, 0, by_z).wait_send()

        @pl.when(b == last)
        def _():
            down_copy(1, b, 0, by_z).wait_send()

    def packed_step(step):
        upto, ahead, over_x, home, adds = step
        code = upto
        code = code * 4 + (ahead[0] + 1 if ahead else 0)
        code = code * 4 + (ahead[1] if ahead else 0)
        code = code * 8 + (over_x[0] + 1 if over_x else 0)
        code = code * 8 + (0 if home is None else home + 1)
        return code * 2 + adds

    steps = jnp.where(at_edge, len(EDGE_STEPS), len(INNER_STEPS))

    def step(i, done):
        code = jnp.where(
            at_edge,
            chosen(i, [packed_step(step) for step in EDGE_STEPS]),
            chosen(i, [packed_step(step) for step in INNER_STEPS]),
        )
        adds = code % 2
        b_slot = code // 2 % 8 - 1
        a_slot = code // 16 % 8 - 1
        f_slot = code // 128 % 4
        q = code // 512 % 4 - 1
        upto = code // 2048 * pieces // 4
        lax.fori_loop(done, upto, receive, 0)

        @pl.when((q == 1) & (f_slot > 0))
        def _():
            over_copy(met(f_slot), everything).wait_recv()

        @pl.when(q >= 0)
        def _():
            forward(q, f_slot)
            swap_copy(q, f_slot).start()

        @pl.when(i == 1)
        def _():
            lax.fori_loop(0, plane, fill, 0)
            for distance in range(n):
                found = jnp.float32(0.0)
                for replica in range(n):
                    for move in range(STEPS):
                        meets = (offsets_ref[replica] + move) % n == distance
                        found = found + jnp.where(meets, 1.0, 0.0)
                weights_ref[distance] = found

        def one_across(part, _):
            across(a_slot, part)
            return 0

        lax.fori_loop(0, jnp.where(a_slot >= 0, 2, 0), one_across, 0)

        @pl.when(b_slot >= 0)
        def _():
            backward(b_slot)

        @pl.when(adds == 1)
        def _():
            margin_terms()

        return upto

    lax.fori_loop(0, steps, step, jnp.int32(0))

    for q in range(2):
        swap_copy(q, jnp.where(at_edge, n - 2, last)).wait_send()

    orbitals_sent()
    gram_all[me] = gram_out[...]
    every_gram().wait_recv()
    whole = gram_all[0]
    for k in range(1, n * n):
        whole = whole + gram_all[k]
    line = jnp.sum(square[...], axis=0, keepdims=True) * weight_of(b, met(2))
    whole = whole + jnp.where((row == b * n + b) & at_edge, line, 0.0)
    sums = jnp.sum(whole, axis=1, keepdims=True) / float(NG**6)
    at_row = lax.broadcasted_iota(jnp.int32, (n * n, n), 0)
    at_lane = lax.broadcasted_iota(jnp.int32, (n * n, n), 1)
    kept = jnp.where(at_row == b * n + at_lane, sums, 0.0)
    margin_ref[...] = jnp.sum(kept, axis=0, keepdims=True)

    @pl.when(at_edge)
    def _():
        term_copy().wait_recv()
        exchanged_ref[...] += term_in[...]

    @pl.when(jnp.logical_not(at_edge))
    def _():
        term_copy().wait_send()

    every_gram().wait_send()


def out_kernel(exchanged_ref, margin_ref, exchanged_out, margin_out, sems):
    copies = [
        pltpu.make_async_copy(exchanged_ref, exchanged_out, sems.at[0]),
        pltpu.make_async_copy(margin_ref, margin_out, sems.at[1]),
    ]
    for copy in copies:
        copy.start()
    for copy in copies:
        copy.wait()


def local_distances(orbitals, offsets):
    n = lax.axis_size("blk")
    pieces = 4
    shared = 1
    rows = orbitals.shape[1] // LANES
    slab = rows // n
    plane = NG * NG // LANES
    tables = cas_tables(NG)
    f32 = jnp.float32
    vmem = pl.BlockSpec(memory_space=pltpu.VMEM)
    dma = pltpu.SemaphoreType.DMA
    operands = [
        pltpu.with_memory_space_constraint(value, pltpu.HBM)
        for value in (offsets, orbitals.reshape(rows, LANES), *tables)
    ]
    exchanged, margin = pl.pallas_call(
        functools.partial(exchange_kernel, n, pieces, shared),
        out_shape=(
            jax.ShapeDtypeStruct((slab, LANES), f32),
            jax.ShapeDtypeStruct((1, n), f32),
        ),
        in_specs=[pl.BlockSpec(memory_space=pltpu.HBM)] * len(operands),
        out_specs=(vmem, vmem),
        scratch_shapes=[
            pltpu.VMEM((2, n, slab, LANES), f32),
            pltpu.VMEM((n, rows, LANES), f32),
            pltpu.VMEM((slab, LANES), f32),
            pltpu.VMEM((n, slab, LANES), f32),
            pltpu.VMEM((plane * NG, LANES), f32),
            pltpu.VMEM((8, LANES), f32),
            pltpu.VMEM((slab, LANES), f32),
            pltpu.VMEM((slab, LANES), f32),
            pltpu.VMEM((n * n, LANES), f32),
            pltpu.VMEM((n * n, n * n, LANES), f32),
            *[pltpu.VMEM(t.shape, t.dtype) for t in tables],
            pltpu.SMEM(offsets.shape, jnp.int32),
            pltpu.SMEM((n,), f32),
            dma((7,)),
            dma((2, n)),
            dma((2, n)),
            dma((n,)),
            dma((n, pieces)),
            dma((n,)),
            dma((n, 2)),
            dma((n, 2)),
            dma((2,)),
            dma((2,)),
        ],
        compiler_params=pltpu.CompilerParams(
            collective_id=0, has_side_effects=True, vmem_limit_bytes=32 << 20
        ),
    )(*operands)
    exchanged, margin = pl.pallas_call(
        out_kernel,
        out_shape=(
            jax.ShapeDtypeStruct((slab, LANES), f32),
            jax.ShapeDtypeStruct((1, n), f32),
        ),
        in_specs=[vmem, vmem],
        out_specs=(pl.BlockSpec(memory_space=pltpu.HBM),) * 2,
        scratch_shapes=[dma((2,))],
    )(*[pltpu.with_memory_space_constraint(value, pltpu.VMEM) for value in (exchanged, margin)])
    return exchanged.reshape(1, slab * LANES), margin


def solution(mesh):
    placed = (P(("groups", "blk"), None), P("groups"))
    paired = mesh.shape["blk"] == mesh.shape["rep"] == 4
    local = local_distances if paired else local_steps
    return jax.shard_map(
        local,
        mesh=mesh,
        in_specs=placed,
        out_specs=(P(("groups", "blk"), "rep"), P(("groups", "blk"), None)),
        check_vma=False,
    )
```
